512 devices in a mesh: ctx: 64 (over z_lo, y, core), tp: 8 (over z_hi, x).
Axes of the slice: x: 4, y: 8, z: 8 (z_hi: 2, z_lo: 4; z = z_hi * 4 + z_lo), core: 2. Of those that a mesh axis runs over, the one named last changes fastest.
Arguments:
- hidden_in: bfloat16 [16384, 2048], P('ctx', 'tp'), may hold values from -6 to 6
- ln_gain: float32 [2048], replicated, may hold values from 0.1 to 1.9
- ln_bias: float32 [2048], replicated, may hold values from -3 to 3
- w_qkv: bfloat16 [3, 2048, 2048], P(None, None, 'tp')
- w_out: bfloat16 [2048, 2048], P('tp'), may hold values from -0.375 to 0.375
- segment_ids: int32 [16384], P('ctx'), may hold values from 0 to 2, as said below
- prompt_lengths: int32 [3], replicated, may hold values from 1 to 8192, as said below
- page_table: int32 [3, 64], replicated, may hold values from -1 to 319, as said below
Outputs:
- attn_out: bfloat16 [16384, 2048], P('ctx', 'tp')
- kv_cache: bfloat16 [320, 128, 2, 2048], P('ctx', None, None, 'tp')
The draws below stay inside these ranges and needn't reach their ends.
Inputs may be any that keep to these rules, and one draw needn't show every extreme that they name: `segment_ids`: each prompt's tokens are consecutive and the numbers never fall along the tokens; prompt i holds exactly prompt_lengths[i] tokens. `prompt_lengths`: the lengths sum to 16384; prompt 0 is shorter than 256 tokens and not a multiple of 128; prompt 1 is the longest, exactly 8192 tokens. `page_table`: for page j of prompt i with j * 128 below prompt_lengths[i], the entry is owner * 5 + slot with slot below 5, where owner is the ctx index whose tokens include the page's first token, starts_i + j * 128; distinct pages have distinct entries; all other entries are -1.
All inputs are finite; a program needn't handle non-finite values.
Results may differ from the reference program's by a relative error of at most 0.013.
Values may be sent and summed in bfloat16 or wider, within the bound.
A program may use at most 128 MiB of HBM per device.

```python
import math
import jax
import jax.numpy as jnp
from jax import lax

D = 2048
H = 8
HD = 256
TOK_DEV = 256
PAGE = 128
NSEG = 3
SPAN = 32
TOKENS = 16384
MAXPAGES = 64
SLOTS = 5
CACHE_SLOTS = 320
N_CTX = 64
N_TP = 8


def segment_layout(key):
    base_key = jax.random.fold_in(key, 101)
    longest = SPAN * TOK_DEV
    whole_pages = jax.random.randint(jax.random.fold_in(base_key, 1), (), 0, TOK_DEV // PAGE).astype(jnp.int32)
    extra_part = jax.random.randint(jax.random.fold_in(base_key, 2), (), 1, PAGE).astype(jnp.int32)
    first_length = (whole_pages * PAGE + extra_part).astype(jnp.int32)
    starts = jnp.stack([jnp.zeros((), jnp.int32), first_length, first_length + longest]).astype(jnp.int32)
    finish = jnp.concatenate([starts[1:], jnp.full((1,), TOKENS, jnp.int32)])
    lengths = (finish - starts).astype(jnp.int32)
    token_index = jnp.arange(TOKENS, dtype=jnp.int32)
    segment_ids = (jnp.sum((starts[None, :] <= token_index[:, None]).astype(jnp.int32), axis=1) - 1).astype(jnp.int32)
    page_index = jnp.arange(MAXPAGES, dtype=jnp.int32)
    page_first = starts[:, None] + page_index[None, :] * PAGE
    is_valid = page_index[None, :] * PAGE < lengths[:, None]
    page_owner = page_first // TOK_DEV
    flat_first = page_first.reshape(-1)
    flat_owner = page_owner.reshape(-1)
    flat_valid = is_valid.reshape(-1)
    earlier = flat_valid[None, :] & (flat_owner[None, :] == flat_owner[:, None]) & (flat_first[None, :] < flat_first[:, None])
    page_rank = jnp.sum(earlier.astype(jnp.int32), axis=1)
    orders = jax.vmap(lambda subkey: jax.random.permutation(subkey, SLOTS))(jax.random.split(jax.random.fold_in(base_key, 3), N_CTX)).astype(jnp.int32)
    slot_pick = orders[jnp.clip(flat_owner, 0, N_CTX - 1), jnp.clip(page_rank, 0, SLOTS - 1)]
    page_map = jnp.where(flat_valid, flat_owner * SLOTS + slot_pick, -1).astype(jnp.int32).reshape(NSEG, MAXPAGES)
    return (segment_ids, lengths, page_map)


def draw_segment_ids(key, part):
    return segment_layout(key)[0]


def draw_prompt_lengths(key, part):
    return segment_layout(key)[1]


def draw_page_table(key, part):
    return segment_layout(key)[2]


def draw_w_qkv(key, part):
    drawn_draw = jax.random.normal(jax.random.fold_in(key, 201), (3, D, H * HD), jnp.float32) * D ** (-0.5)
    return drawn_draw.astype(jnp.bfloat16)


def steps_of(own_key, dims, pieces, low, top_value):
    gain = 1.0
    for position, parts in pieces:
        steps = jax.random.uniform(jax.random.fold_in(jax.random.fold_in(own_key, 6), position), (parts,), jnp.float32, low / len(pieces), top_value / len(pieces))
        gain = gain * jnp.repeat(jnp.exp(steps), dims[position] // parts).reshape((-1,) + (1,) * (len(dims) - 1 - position))
    return gain


def centred(key, extent, width, bound, cuts=(), kind=jnp.bfloat16):
    array = jax.random.normal(key, extent, jnp.float32) * width
    if len(cuts) > 0:
        array = steps_of(key, extent, cuts, -0.22, 0.18) * array
    return jnp.clip(array, min=-bound, max=bound).astype(kind)


def setup_inputs(seed: int = 0) -> dict:
    keys = jax.random.split(jax.random.key(seed), 9)
    hidden_in = centred(keys[0], (TOKENS, D), 1.0, 6.0, ((0, 64), (1, 8)))
    ln_gain = jnp.clip(1.0 + 0.18 * jax.random.normal(keys[1], (D,), jnp.float32), 0.1, 1.9)
    ln_bias = centred(keys[2], (D,), 0.5, 3.0, (), jnp.float32)
    w_qkv = draw_w_qkv(jax.random.fold_in(keys[8], 71), 0)
    w_out = centred(keys[4], (H * HD, D), HD ** -0.5, 0.375, ((0, 8),))
    segment_ids = draw_segment_ids(jax.random.fold_in(keys[8], 71), 0)
    prompt_lengths = draw_prompt_lengths(jax.random.fold_in(keys[8], 71), 0)
    page_table = draw_page_table(jax.random.fold_in(keys[8], 71), 0)
    return dict(hidden_in=hidden_in, ln_gain=ln_gain, ln_bias=ln_bias, w_qkv=w_qkv, w_out=w_out, segment_ids=segment_ids, prompt_lengths=prompt_lengths, page_table=page_table)


EPSILON = 1e-05

def normalize(inputs, norm_gain, norm_bias):
    average = lax.optimization_barrier(jnp.sum(inputs, axis=-1, keepdims=True)) / inputs.shape[-1]
    centered = inputs - average
    spread = lax.optimization_barrier(jnp.sum(centered * centered, axis=-1, keepdims=True)) / inputs.shape[-1]
    return centered * lax.rsqrt(spread + EPSILON) * norm_gain + norm_bias

def rotary(inputs, positions):
    quarter = inputs.shape[-1] // 4
    halfway = quarter // 2
    exponent = jnp.arange(0, quarter, 2).astype(jnp.float32) / quarter
    inverse = jnp.power(jnp.float32(10000.0), -exponent)
    angles = positions.astype(jnp.float32)[:, None] * inverse[None, :]
    cosine_table = jnp.concatenate([jnp.cos(angles), jnp.cos(angles)], axis=-1)[:, None, :]
    sine_table = jnp.concatenate([jnp.sin(angles), jnp.sin(angles)], axis=-1)[:, None, :]
    leading = inputs[..., :quarter]
    turned = jnp.concatenate([-leading[..., halfway:], leading[..., :halfway]], axis=-1)
    return jnp.concatenate([leading * cosine_table + turned * sine_table, inputs[..., quarter:]], axis=-1)

def reference(hidden_in, ln_gain, ln_bias, w_qkv, w_out, segment_ids, prompt_lengths, page_table):
    normed = normalize(hidden_in.astype(jnp.float32), ln_gain, ln_bias).astype(jnp.bfloat16)
    starts = (jnp.cumsum(prompt_lengths) - prompt_lengths).astype(jnp.int32)
    positions = (jnp.arange(TOKENS, dtype=jnp.int32) - starts[segment_ids]).astype(jnp.int32)
    query_heads = rotary(jnp.dot(normed, w_qkv[0], preferred_element_type=jnp.float32).reshape(TOKENS, H, HD), positions).astype(jnp.bfloat16)
    key_heads = rotary(jnp.dot(normed, w_qkv[1], preferred_element_type=jnp.float32).reshape(TOKENS, H, HD), positions).astype(jnp.bfloat16)
    value_heads = jnp.dot(normed, w_qkv[2], preferred_element_type=jnp.float32).reshape(TOKENS, H, HD).astype(jnp.bfloat16)
    reach_rows = SPAN * TOK_DEV
    padded_keys = jnp.concatenate([jnp.zeros((reach_rows, H, HD), jnp.bfloat16), key_heads], axis=0)
    padded_values = jnp.concatenate([jnp.zeros((reach_rows, H, HD), jnp.bfloat16), value_heads], axis=0)
    padded_marks = jnp.concatenate([jnp.full((reach_rows,), -1, jnp.int32), segment_ids], axis=0)

    def attend_block(block_number):
        first_row = (block_number * TOK_DEV).astype(jnp.int32)
        query_block = lax.dynamic_slice_in_dim(query_heads, first_row, TOK_DEV, 0).astype(jnp.float32)
        query_marks = lax.dynamic_slice_in_dim(segment_ids, first_row, TOK_DEV, 0)
        key_block = lax.dynamic_slice_in_dim(padded_keys, first_row, reach_rows + TOK_DEV, 0).astype(jnp.float32)
        value_block = lax.dynamic_slice_in_dim(padded_values, first_row, reach_rows + TOK_DEV, 0).astype(jnp.float32)
        key_marks = lax.dynamic_slice_in_dim(padded_marks, first_row, reach_rows + TOK_DEV, 0)
        query_index = first_row + jnp.arange(TOK_DEV, dtype=jnp.int32)
        key_index = first_row - reach_rows + jnp.arange(reach_rows + TOK_DEV, dtype=jnp.int32)
        visible = (query_marks[:, None] == key_marks[None, :]) & (key_index[None, :] <= query_index[:, None])
        scores = jnp.einsum('qhd,khd->hqk', query_block, key_block) / math.sqrt(HD)
        scores = jnp.where(visible[None], scores, -jnp.inf)
        row_peak = lax.optimization_barrier(jnp.max(scores, axis=-1, keepdims=True))
        weights = jnp.exp(scores - row_peak).astype(jnp.bfloat16)
        weights = lax.optimization_barrier(weights).astype(jnp.float32)
        totals = lax.optimization_barrier(jnp.sum(weights, axis=-1))
        mixture = jnp.einsum('hqk,khd->hqd', weights, value_block) / totals[..., None]
        return jnp.transpose(mixture, (1, 0, 2)).astype(jnp.bfloat16)
    attended = lax.map(attend_block, jnp.arange(N_CTX, dtype=jnp.int32)).reshape(TOKENS, H * HD)
    group_width = H // N_TP * HD
    accumulated = jnp.zeros((TOKENS, D), jnp.float32)
    for member in range(N_TP):
        partial_value = jnp.dot(attended[:, member * group_width:(member + 1) * group_width], w_out[member * group_width:(member + 1) * group_width], preferred_element_type=jnp.float32).astype(jnp.bfloat16)
        accumulated = accumulated + lax.optimization_barrier(partial_value).astype(jnp.float32)
    attn_out = accumulated.astype(jnp.bfloat16)
    page_slot = page_table[segment_ids, positions // PAGE]
    offsets = positions % PAGE
    kv_cache = jnp.zeros((CACHE_SLOTS, PAGE, 2, H * HD), jnp.bfloat16)
    kv_cache = kv_cache.at[page_slot, offsets, 0].set(key_heads.reshape(TOKENS, H * HD))
    kv_cache = kv_cache.at[page_slot, offsets, 1].set(value_heads.reshape(TOKENS, H * HD))
    return (attn_out, kv_cache)
```

```python
import jax
import jax.numpy as jnp
from jax import lax
from jax.experimental import pallas as pl
from jax.experimental.pallas import tpu as pltpu
from jax.sharding import PartitionSpec as P

HD = 256
PAGE = 128
ROWS = 256
GROUP = 32
EPSILON = 1e-05
MESH = pl.DeviceIdType.MESH
F32 = jnp.float32
BF16 = jnp.bfloat16

OFFSETS = (0, -1, 1, 0, -2, 2, -1, 1, -3, 3, -2, 2, 4, -3, 3, -4)
CROSS = (3, 6, 7, 10, 11, 13, 14, 15)


def pick(step, table):
    value = 0
    for place, entry in enumerate(table):
        if entry != 0:
            value = value + jnp.where(step == place, entry, 0)
    return value


def among(step, places):
    found = step == places[0]
    for place in places[1:]:
        found = found | (step == place)
    return found


def remote(src, dst, send, recv, **where):
    return pltpu.make_async_remote_copy(
        src_ref=src, dst_ref=dst, send_sem=send, recv_sem=recv, device_id=where, device_id_type=MESH
    )


def kernel(
    lengths, pages, hidden, gain, bias, cosine, sine, w_qkv, w_out,
    out, cache,
    gathered, normed, w_qkv_v, w_out_v, queries, pairs, every, best, total, acc,
    helped, attended, terms, first, second, last,
    local_sem, ag_send, ag_recv, kv_send, kv_recv, extra_send, extra_recv, rs_send, rs_recv,
):
    ctx = lax.axis_index("ctx")
    tp = lax.axis_index("tp")
    group = ctx // GROUP
    local = ctx % GROUP
    z = local // 16
    y = (local // 2) % 8
    core = local % 2
    base = group * GROUP
    half = tp // 4
    x = tp % 4
    up = base + z * 16 + ((y + 1) % 8) * 2 + core
    down = base + z * 16 + ((y + 7) % 8) * 2 + core
    twin = base + z * 16 + y * 2 + (1 - core)
    across = base + (1 - z) * 16 + y * 2 + core
    x_up = half * 4 + (x + 1) % 4
    x_down = half * 4 + (x + 3) % 4
    x_far = half * 4 + (x + 2) % 4
    mirror = (1 - half) * 4 + x
    is_helper = ctx == 16
    is_helped = ctx == 32

    copies_in = [
        pltpu.make_async_copy(w_qkv, w_qkv_v, local_sem.at[0]),
        pltpu.make_async_copy(w_out, w_out_v, local_sem.at[1]),
    ]
    for copy in copies_in:
        copy.start()

    barrier = pltpu.get_barrier_semaphore()
    for peer in (up, down, twin, across):
        pl.semaphore_signal(barrier, inc=1, device_id={"ctx": peer}, device_id_type=MESH)
    for peer in (x_up, x_down, mirror):
        pl.semaphore_signal(barrier, inc=1, device_id={"tp": peer}, device_id_type=MESH)

    @pl.when(ctx > 0)
    def _():
        pl.semaphore_signal(barrier, inc=1, device_id={"ctx": ctx - 1}, device_id_type=MESH)

    @pl.when(ctx < 63)
    def _():
        pl.semaphore_signal(barrier, inc=1, device_id={"ctx": ctx + 1}, device_id_type=MESH)

    @pl.when(is_helper | is_helped)
    def _():
        pl.semaphore_signal(barrier, inc=1, device_id={"ctx": 48 - ctx}, device_id_type=MESH)

    pl.semaphore_wait(
        barrier,
        7 + jnp.where(ctx > 0, 1, 0) + jnp.where(ctx < 63, 1, 0)
        + jnp.where(is_helper | is_helped, 1, 0),
    )

    top, bottom = pl.ds(0, 128), pl.ds(128, 128)

    def feature_copy(number, src, slot, part, peer, rows=None):
        dst = gathered.at[slot] if rows is None else gathered.at[slot, rows]
        return remote(src, dst, ag_send.at[number], ag_recv.at[slot, part], tp=peer)

    own_z = feature_copy(0, hidden, tp, 0, mirror)
    own_up = feature_copy(1, hidden, tp, 0, x_up)
    own_down = feature_copy(2, hidden, tp, 0, x_down)
    for copy in (own_z, own_up, own_down):
        copy.start()
    gathered[tp] = hidden[...]
    sent = [own_z, own_up, own_down]

    def arrived(slot, part, rows=None):
        dst = gathered.at[slot] if rows is None else gathered.at[slot, rows]
        remote(dst, dst, ag_send.at[0], ag_recv.at[slot, part], tp=mirror).wait_recv()

    def pass_on(slot_down, slot_up, number):
        arrived(slot_down, 0)
        one = feature_copy(number, gathered.at[slot_down, top], slot_down, 0, x_up, top)
        one.start()
        arrived(slot_up, 0)
        two = feature_copy(number + 1, gathered.at[slot_up, bottom], slot_up, 1, x_down, bottom)
        two.start()
        sent.extend([one, two])

    pass_on(x_down, x_up, 3)
    other = (1 - half) * 4
    arrived(mirror, 0)
    cross_up = feature_copy(5, gathered.at[mirror], mirror, 0, x_up)
    cross_down = feature_copy(6, gathered.at[mirror], mirror, 0, x_down)
    cross_up.start()
    cross_down.start()
    sent.extend([cross_up, cross_down])
    arrived(x_far, 0, top)
    arrived(x_far, 1, bottom)
    pass_on(other + (x + 3) % 4, other + (x + 1) % 4, 7)
    arrived(other + (x + 2) % 4, 0, top)
    arrived(other + (x + 2) % 4, 1, bottom)
    for copy in sent:
        copy.wait_send()

    @pl.loop(0, ROWS // 32)
    def _(step):
        rows = pl.ds(pl.multiple_of(step * 32, 32), 32)
        blocks = [gathered[b, rows, :].astype(F32) for b in range(8)]
        average = jnp.sum(sum(blocks), axis=-1, keepdims=True) / 2048
        centered = [block - average for block in blocks]
        spread = jnp.sum(sum(c * c for c in centered), axis=-1, keepdims=True) / 2048
        scale = lax.rsqrt(spread + EPSILON)
        for b in range(8):
            cols = pl.ds(b * 256, 256)
            value = centered[b] * scale * gain[:, cols] + bias[:, cols]
            normed[rows, cols] = value.astype(BF16)

    copies_in[0].wait()
    lane = lax.broadcasted_iota(jnp.int32, (ROWS, 128), 1)

    def turn(value):
        lead = value[:, :128]
        turned = jnp.where(lane < 32, pltpu.roll(lead, 96, 1), pltpu.roll(lead, 32, 1))
        lead = lead * cosine[...] + turned * sine[...]
        return jnp.concatenate([lead, value[:, 128:]], axis=1).astype(BF16)

    key = turn(jnp.dot(normed[...], w_qkv_v[1], preferred_element_type=F32))
    pairs[local, :, 0:256] = key
    every[0:256, 0:256] = key
    value = jnp.dot(normed[...], w_qkv_v[2], preferred_element_type=F32).astype(BF16)
    pairs[local, :, 256:512] = value
    every[0:256, 256:512] = value

    def pair_copy(way, slot, peer):
        return remote(
            pairs.at[slot], pairs.at[slot], kv_send.at[way, slot], kv_recv.at[slot], ctx=peer
        )

    pair_copy(0, local, up).start()
    pair_copy(1, local, down).start()

    @pl.when(z == 0)
    def _():
        pair_copy(2, local, across).start()

    pair_copy(3, local, twin).start()
    tail = remote(
        pairs.at[local, pl.ds(0, PAGE)], every.at[pl.ds(256, PAGE)],
        extra_send.at[0], extra_recv.at[0], ctx=jnp.maximum(ctx - 1, 0),
    )

    @pl.when(ctx > 0)
    def _():
        tail.start()

    query = turn(jnp.dot(normed[...], w_qkv_v[0], preferred_element_type=F32))
    queries[0] = query * jnp.asarray(1 / 16, BF16)

    ask = remote(queries.at[0], queries.at[1], extra_send.at[1], extra_recv.at[1], ctx=16)
    show = remote(pairs.at[local], pairs.at[GROUP], extra_send.at[2], extra_recv.at[2], ctx=16)
    give = remote(helped.at[0], helped.at[1], extra_send.at[3], extra_recv.at[3], ctx=32)

    @pl.when(is_helped)
    def _():
        ask.start()
        show.start()

    best[...] = jnp.full(best.shape, -jnp.inf, F32)
    total[...] = jnp.zeros(total.shape, F32)
    acc[...] = jnp.zeros(acc.shape, F32)
    length = lengths[0]
    q_place = lax.broadcasted_iota(jnp.int32, (ROWS, ROWS), 0)
    k_place = lax.broadcasted_iota(jnp.int32, (ROWS, ROWS), 1)

    def attend(which, slot, visible):
        scores = lax.dot_general(
            queries[which], pairs[slot, :, 0:256], (((1,), (1,)), ((), ())),
            preferred_element_type=F32,
        )
        scores = jnp.where(visible, scores, -jnp.inf)
        before = best[which]
        newest = jnp.maximum(before, jnp.max(scores, axis=-1, keepdims=True))
        rescale = jnp.exp(before - newest)
        weights = jnp.exp(scores - jnp.concatenate([newest, newest], axis=1)).astype(BF16)
        total[which] = total[which] * rescale + jnp.sum(
            weights.astype(F32), axis=-1, keepdims=True
        )
        acc[which] = acc[which] * jnp.concatenate([rescale, rescale], axis=1) + jnp.dot(
            weights, pairs[slot, :, 256:512], preferred_element_type=F32
        )
        best[which] = newest

    def visit(slot):
        bound = jnp.where(slot == 0, length, 0)

        def one(which, carry):
            attend(which, slot, k_place >= bound)
            return carry

        lax.fori_loop(
            jnp.where(slot < local, 0, 1), jnp.where(is_helper, 2, 1), one, 0
        )

    own_bound = jnp.where(local == 0, length, 0)
    causal = k_place <= q_place
    attend(0, local, causal & ((k_place >= own_bound) == (q_place >= own_bound)))

    def here(slot):
        pair_copy(0, slot, up).wait_recv()

    @pl.when(is_helper)
    def _():
        ask.wait_recv()
        show.wait_recv()
        attend(1, GROUP, causal)
        visit(local)

    @pl.when(ctx < 63)
    def _():
        tail.wait_recv()

    @pl.when(ctx == 63)
    def _():
        every[256:384, :] = jnp.zeros((PAGE, 512), BF16)

    shifts = [0] * 5
    counts = [0] * 5
    start = 0
    token = ctx * ROWS
    for prompt in range(3):
        size = lengths[prompt]
        head = jnp.maximum(token - start + PAGE - 1, 0) // PAGE
        for number in range(2):
            page = head + number
            row = start + page * PAGE - token
            valid = (row < ROWS) & (page * PAGE < size)
            entry = pages[prompt, jnp.minimum(page, 63)] % 5
            for slot in range(5):
                hit = valid & (entry == slot)
                shifts[slot] = shifts[slot] + jnp.where(hit, row, 0)
                counts[slot] = counts[slot] + jnp.where(hit, jnp.minimum(size - page * PAGE, PAGE), 0)
        start = start + size
    to_row = lax.broadcasted_iota(jnp.int32, (PAGE, 384), 0)
    from_row = lax.broadcasted_iota(jnp.int32, (PAGE, 384), 1)
    for slot in range(5):
        placing = (from_row == to_row + shifts[slot]) & (to_row < counts[slot])
        placing = jnp.where(placing, 1.0, 0.0).astype(BF16)
        cache[slot] = jnp.dot(placing, every[...], preferred_element_type=F32).astype(BF16)

    here(local + 1 - 2 * core)
    visit(local + 1 - 2 * core)

    def event(step, carry):
        crossing = among(step, CROSS)
        row = jnp.where(crossing, 0, z)
        spot = row * 16 + ((y + pick(step, OFFSETS) + 8) % 8) * 2

        @pl.when((z == 1) | jnp.logical_not(crossing))
        def _():
            slot = spot + core
            here(slot)

            @pl.when(goes_up(step))
            def _():
                pair_copy(0, slot, up).start()

            @pl.when(goes_down(step))
            def _():
                pair_copy(1, slot, down).start()

            @pl.when(goes_across(step))
            def _():
                pair_copy(2, slot, across).start()

            pair_copy(3, slot, twin).start()
            visit(slot)
            beside = spot + 1 - core
            here(beside)
            visit(beside)

        return carry

    def goes_up(step):
        return among(step, (1, 4, 10, 13)) | ((step == 8) & (z == 0))

    def goes_down(step):
        return among(step, (2, 5, 11)) | ((step == 9) & (z == 1))

    def goes_across(step):
        return among(step, (1, 2, 4, 5)) & (z == 0)

    lax.fori_loop(1, 16, event, 0)

    @pl.when(is_helper)
    def _():
        helped[0] = (acc[1] / jnp.concatenate([total[1], total[1]], axis=1)).astype(BF16)
        give.start()

    result = (acc[0] / jnp.concatenate([total[0], total[0]], axis=1)).astype(BF16)
    attended[...] = result

    @pl.when(is_helped)
    def _():
        give.wait_recv()
        rows = lax.broadcasted_iota(jnp.int32, (ROWS, 256), 0)
        merged = jnp.where(rows < length, helped[1].astype(F32), attended[...].astype(F32))
        attended[...] = merged.astype(BF16)

    copies_in[1].wait()

    @pl.loop(0, 8)
    def _(b):
        cols = pl.ds(pl.multiple_of(b * 256, 256), 256)
        terms[b] = jnp.dot(
            attended[...], w_out_v[:, cols], preferred_element_type=F32
        ).astype(BF16)

    def sum_copy(number, src, dst, peer):
        return remote(src, dst, rs_send.at[number], rs_recv.at[number], tp=peer)

    first_ups, first_downs = [], []
    for k in range(2):
        side = (1 - half if k == 0 else half) * 4
        far = side + (x + 2) % 4
        first_ups.append(sum_copy(4 * k, terms.at[far, top], first.at[k, top], x_up))
        first_downs.append(
            sum_copy(4 * k + 1, terms.at[far, bottom], first.at[k, bottom], x_down)
        )
        first_ups[k].start()
        first_downs[k].start()
    seconds = []
    for k in range(2):
        side = (1 - half if k == 0 else half) * 4
        to_up, to_down = side + (x + 1) % 4, side + (x + 3) % 4
        first_ups[k].wait_recv()
        terms[to_up, top] = (
            terms[to_up, top].astype(F32) + first[k, top].astype(F32)
        ).astype(BF16)
        one = sum_copy(4 * k + 2, terms.at[to_up], second.at[k, 0], x_up)
        one.start()
        first_downs[k].wait_recv()
        terms[to_down, bottom] = (
            terms[to_down, bottom].astype(F32) + first[k, bottom].astype(F32)
        ).astype(BF16)
        two = sum_copy(4 * k + 3, terms.at[to_down], second.at[k, 1], x_down)
        two.start()
        seconds.append((one, two))

    def summed(k):
        side = (1 - half if k == 0 else half) * 4
        for copy in seconds[k]:
            copy.wait_recv()
        return (
            terms[side + x].astype(F32) + second[k, 0].astype(F32) + second[k, 1].astype(F32)
        )

    last[0] = summed(0).astype(BF16)
    final = sum_copy(8, last.at[0], last.at[1], mirror)
    final.start()
    kept = summed(1)
    final.wait_recv()
    out[...] = (kept + last[1].astype(F32)).astype(BF16)

    for copy in first_ups + first_downs + [c for pair in seconds for c in pair] + [final]:
        copy.wait_send()

    @pl.when(ctx > 0)
    def _():
        tail.wait_send()

    @pl.when(is_helped)
    def _():
        ask.wait_send()
        show.wait_send()

    @pl.when(is_helper)
    def _():
        give.wait_send()

    pair_copy(0, local, up).wait_send()
    pair_copy(1, local, down).wait_send()

    @pl.when(z == 0)
    def _():
        pair_copy(2, local, across).wait_send()

    pair_copy(3, local, twin).wait_send()

    def drain(step, carry):
        crossing = among(step, CROSS)
        row = jnp.where(crossing, 0, z)
        slot = row * 16 + ((y + pick(step, OFFSETS) + 8) % 8) * 2 + core

        @pl.when((z == 1) | jnp.logical_not(crossing))
        def _():
            @pl.when(goes_up(step))
            def _():
                pair_copy(0, slot, up).wait_send()

            @pl.when(goes_down(step))
            def _():
                pair_copy(1, slot, down).wait_send()

            @pl.when(goes_across(step))
            def _():
                pair_copy(2, slot, across).wait_send()

            pair_copy(3, slot, twin).wait_send()

        return carry

    lax.fori_loop(1, 16, drain, 0)


def rotary_tables(prompt_lengths):
    quarter = HD // 4
    exponent = jnp.arange(0, quarter, 2).astype(F32) / quarter
    inverse = jnp.power(F32(10000.0), -exponent)
    index = lax.axis_index("ctx") * ROWS + jnp.arange(ROWS, dtype=jnp.int32)
    first, both = prompt_lengths[0], prompt_lengths[0] + prompt_lengths[1]
    start = jnp.where(index < first, 0, jnp.where(index < both, first, both))
    angles = (index - start).astype(F32)[:, None] * inverse[None, :]
    cosine, sine = jnp.cos(angles), jnp.sin(angles)
    ones, zeros = jnp.ones((ROWS, 64), F32), jnp.zeros((ROWS, 64), F32)
    return (
        jnp.concatenate([cosine, cosine, ones], axis=1),
        jnp.concatenate([-sine, sine, zeros], axis=1),
    )


def per_device(hidden_in, ln_gain, ln_bias, w_qkv, w_out, segment_ids, prompt_lengths, page_table):
    cosine, sine = rotary_tables(prompt_lengths)
    vmem = pl.BlockSpec(memory_space=pltpu.VMEM)
    smem = pl.BlockSpec(memory_space=pltpu.SMEM)
    held = pl.BlockSpec(memory_space=pl.ANY)
    dma = pltpu.SemaphoreType.DMA
    attn_out, cache = pl.pallas_call(
        kernel,
        out_shape=(
            jax.ShapeDtypeStruct((ROWS, 256), BF16),
            jax.ShapeDtypeStruct((5, PAGE, 512), BF16),
        ),
        in_specs=[smem, smem, vmem, vmem, vmem, vmem, vmem, held, held],
        out_specs=(vmem, vmem),
        scratch_shapes=[
            pltpu.VMEM((8, ROWS, 256), BF16),
            pltpu.VMEM((ROWS, 2048), BF16),
            pltpu.VMEM((3, 2048, 256), BF16),
            pltpu.VMEM((256, 2048), BF16),
            pltpu.VMEM((2, ROWS, 256), BF16),
            pltpu.VMEM((GROUP + 1, ROWS, 512), BF16),
            pltpu.VMEM((384, 512), BF16),
            pltpu.VMEM((2, ROWS, 128), F32),
            pltpu.VMEM((2, ROWS, 128), F32),
            pltpu.VMEM((2, ROWS, 256), F32),
            pltpu.VMEM((2, ROWS, 256), BF16),
            pltpu.VMEM((ROWS, 256), BF16),
            pltpu.VMEM((8, ROWS, 256), BF16),
            pltpu.VMEM((2, ROWS, 256), BF16),
            pltpu.VMEM((2, 2, ROWS, 256), BF16),
            pltpu.VMEM((2, ROWS, 256), BF16),
            dma((2,)),
            dma((9,)),
            dma((8, 2)),
            dma((4, GROUP)),
            dma((GROUP,)),
            dma((4,)),
            dma((4,)),
            dma((9,)),
            dma((9,)),
        ],
        compiler_params=pltpu.CompilerParams(
            collective_id=0, has_side_effects=True, vmem_limit_bytes=44 * 1024 * 1024
        ),
    )(
        prompt_lengths, page_table, hidden_in, ln_gain.reshape(1, -1), ln_bias.reshape(1, -1),
        cosine, sine, w_qkv, w_out,
    )
    return (attn_out, cache.reshape(5, PAGE, 2, 256))


def solution(mesh):
    return jax.shard_map(
        per_device,
        mesh=mesh,
        in_specs=(P("ctx", "tp"), P(), P(), P(None, None, "tp"), P("tp", None), P("ctx"), P(), P()),
        out_specs=(P("ctx", "tp"), P("ctx", None, None, "tp")),
        check_vma=False,
    )
```

```python
import jax
import numpy as np
import jax.numpy as jnp
from jax import lax
from jax.experimental import pallas as pl
from jax.experimental.pallas import tpu as pltpu
from jax.sharding import PartitionSpec as P

HD = 256
PAGE = 128
ROWS = 256
GROUP = 32
EPSILON = 1e-05
TURN = (6.28125, 0.00193500518798828125, 3.0197e-07)
MESH = pl.DeviceIdType.MESH
F32 = jnp.float32
BF16 = jnp.bfloat16

OFFSETS = (0, -1, 1, 0, -2, 2, -1, 1, -3, 3, -2, 2, 4, -3, 3, -4)
CROSS = (3, 6, 7, 10, 11, 13, 14, 15)


def pick(step, table):
    value = 0
    for place, entry in enumerate(table):
        if entry != 0:
            value = value + jnp.where(step == place, entry, 0)
    return value


def among(step, places):
    found = step == places[0]
    for place in places[1:]:
        found = found | (step == place)
    return found


def remote(src, dst, send, recv, **where):
    return pltpu.make_async_remote_copy(
        src_ref=src, dst_ref=dst, send_sem=send, recv_sem=recv, device_id=where, device_id_type=MESH
    )


def kernel(
    lengths, pages, hidden_h, gain_h, bias_h, inverse_h, w_qkv, w_out,
    out, cache,
    hidden, gain, bias, inverse, cosine, sine, gathered, normed, w_qkv_v, w_out_v, queries, pairs, every, best, total, acc,
    helped, attended, terms, first, second, last,
    local_sem, ag_send, ag_recv, kv_send, kv_recv, extra_send, extra_recv, rs_send, rs_recv,
):
    ctx = lax.axis_index("ctx")
    tp = lax.axis_index("tp")
    group = ctx // GROUP
    local = ctx % GROUP
    z = local // 16
    y = (local // 2) % 8
    core = local % 2
    base = group * GROUP
    half = tp // 4
    x = tp % 4
    up = base + z * 16 + ((y + 1) % 8) * 2 + core
    down = base + z * 16 + ((y + 7) % 8) * 2 + core
    twin = base + z * 16 + y * 2 + (1 - core)
    across = base + (1 - z) * 16 + y * 2 + core
    x_up = half * 4 + (x + 1) % 4
    x_down = half * 4 + (x + 3) % 4
    x_far = half * 4 + (x + 2) % 4
    mirror = (1 - half) * 4 + x
    is_helper = ctx == 16
    is_helped = ctx == 32

    copies_in = [
        pltpu.make_async_copy(source, target, local_sem.at[number])
        for number, (source, target) in enumerate((
            (hidden_h, hidden), (inverse_h, inverse), (gain_h, gain), (bias_h, bias),
            (w_qkv, w_qkv_v), (w_out, w_out_v),
        ))
    ]
    for copy in copies_in:
        copy.start()

    barrier = pltpu.get_barrier_semaphore()
    for peer in (up, down, twin, across):
        pl.semaphore_signal(barrier, inc=1, device_id={"ctx": peer}, device_id_type=MESH)
    for peer in (x_up, x_down, mirror):
        pl.semaphore_signal(barrier, inc=1, device_id={"tp": peer}, device_id_type=MESH)

    @pl.when(ctx > 0)
    def _():
        pl.semaphore_signal(barrier, inc=1, device_id={"ctx": ctx - 1}, device_id_type=MESH)

    @pl.when(ctx < 63)
    def _():
        pl.semaphore_signal(barrier, inc=1, device_id={"ctx": ctx + 1}, device_id_type=MESH)

    @pl.when(is_helper | is_helped)
    def _():
        pl.semaphore_signal(barrier, inc=1, device_id={"ctx": 48 - ctx}, device_id_type=MESH)

    pl.semaphore_wait(
        barrier,
        7 + jnp.where(ctx > 0, 1, 0) + jnp.where(ctx < 63, 1, 0)
        + jnp.where(is_helper | is_helped, 1, 0),
    )

    top, bottom = pl.ds(0, 128), pl.ds(128, 128)

    def feature_copy(number, src, slot, part, peer, rows=None):
        dst = gathered.at[slot] if rows is None else gathered.at[slot, rows]
        return remote(src, dst, ag_send.at[number], ag_recv.at[slot, part], tp=peer)

    copies_in[0].wait()
    own_z = feature_copy(0, hidden, tp, 0, mirror)
    own_up = feature_copy(1, hidden, tp, 0, x_up)
    own_down = feature_copy(2, hidden, tp, 0, x_down)
    for copy in (own_z, own_up, own_down):
        copy.start()
    gathered[tp] = hidden[...]
    sent = [own_z, own_up, own_down]

    copies_in[1].wait()
    index = ctx * ROWS + lax.broadcasted_iota(jnp.int32, (ROWS, 128), 0)
    lane = lax.broadcasted_iota(jnp.int32, (ROWS, 128), 1)
    length = lengths[0]
    both = length + lengths[1]
    places = index - jnp.where(index < length, 0, jnp.where(index < both, length, both))
    angles = places.astype(F32) * inverse[...]
    turns = jnp.floor(angles * F32(0.15915494309189535) + 0.5)
    for part in TURN:
        angles = angles - turns * F32(part)
    cosine[...] = jnp.where(lane < 64, jnp.cos(angles), 1.0)
    sine[...] = jnp.where(
        lane < 32, -jnp.sin(angles), jnp.where(lane < 64, jnp.sin(angles), 0.0)
    )

    def arrived(slot, part, rows=None):
        dst = gathered.at[slot] if rows is None else gathered.at[slot, rows]
        remote(dst, dst, ag_send.at[0], ag_recv.at[slot, part], tp=mirror).wait_recv()

    def pass_on(slot_down, slot_up, number):
        arrived(slot_down, 0)
        one = feature_copy(number, gathered.at[slot_down, top], slot_down, 0, x_up, top)
        one.start()
        arrived(slot_up, 0)
        two = feature_copy(number + 1, gathered.at[slot_up, bottom], slot_up, 1, x_down, bottom)
        two.start()
        sent.extend([one, two])

    pass_on(x_down, x_up, 3)
    other = (1 - half) * 4
    arrived(mirror, 0)
    cross_up = feature_copy(5, gathered.at[mirror], mirror, 0, x_up)
    cross_down = feature_copy(6, gathered.at[mirror], mirror, 0, x_down)
    cross_up.start()
    cross_down.start()
    sent.extend([cross_up, cross_down])
    arrived(x_far, 0, top)
    arrived(x_far, 1, bottom)
    pass_on(other + (x + 3) % 4, other + (x + 1) % 4, 7)
    arrived(other + (x + 2) % 4, 0, top)
    arrived(other + (x + 2) % 4, 1, bottom)
    for copy in sent:
        copy.wait_send()

    copies_in[2].wait()
    copies_in[3].wait()
    @pl.loop(0, ROWS // 32)
    def _(step):
        rows = pl.ds(pl.multiple_of(step * 32, 32), 32)
        blocks = [gathered[b, rows, :].astype(F32) for b in range(8)]
        average = jnp.sum(sum(blocks), axis=-1, keepdims=True) / 2048
        centered = [block - average for block in blocks]
        spread = jnp.sum(sum(c * c for c in centered), axis=-1, keepdims=True) / 2048
        scale = lax.rsqrt(spread + EPSILON)
        for b in range(8):
            cols = pl.ds(b * 256, 256)
            value = centered[b] * scale * gain[:, cols] + bias[:, cols]
            normed[rows, cols] = value.astype(BF16)

    copies_in[4].wait()

    def turn(value):
        lead = value[:, :128]
        turned = jnp.where(lane < 32, pltpu.roll(lead, 96, 1), pltpu.roll(lead, 32, 1))
        lead = lead * cosine[...] + turned * sine[...]
        return jnp.concatenate([lead, value[:, 128:]], axis=1).astype(BF16)

    key = turn(jnp.dot(normed[...], w_qkv_v[1], preferred_element_type=F32))
    pairs[local, :, 0:256] = key
    every[0:256, 0:256] = key
    value = jnp.dot(normed[...], w_qkv_v[2], preferred_element_type=F32).astype(BF16)
    pairs[local, :, 256:512] = value
    every[0:256, 256:512] = value

    def pair_copy(way, slot, peer):
        return remote(
            pairs.at[slot], pairs.at[slot], kv_send.at[way, slot], kv_recv.at[slot], ctx=peer
        )

    pair_copy(0, local, up).start()
    pair_copy(1, local, down).start()

    @pl.when(z == 0)
    def _():
        pair_copy(2, local, across).start()

    pair_copy(3, local, twin).start()
    tail = remote(
        pairs.at[local, pl.ds(0, PAGE)], every.at[pl.ds(256, PAGE)],
        extra_send.at[0], extra_recv.at[0], ctx=jnp.maximum(ctx - 1, 0),
    )

    @pl.when(ctx > 0)
    def _():
        tail.start()

    query = turn(jnp.dot(normed[...], w_qkv_v[0], preferred_element_type=F32))
    queries[0] = query * jnp.asarray(1 / 16, BF16)

    ask = remote(queries.at[0], queries.at[1], extra_send.at[1], extra_recv.at[1], ctx=16)
    show = remote(pairs.at[local], pairs.at[GROUP], extra_send.at[2], extra_recv.at[2], ctx=16)
    give = remote(helped.at[0], helped.at[1], extra_send.at[3], extra_recv.at[3], ctx=32)

    @pl.when(is_helped)
    def _():
        ask.start()
        show.start()

    best[...] = jnp.full(best.shape, -jnp.inf, F32)
    total[...] = jnp.zeros(total.shape, F32)
    acc[...] = jnp.zeros(acc.shape, F32)
    q_place = lax.broadcasted_iota(jnp.int32, (ROWS, ROWS), 0)
    k_place = lax.broadcasted_iota(jnp.int32, (ROWS, ROWS), 1)

    def attend(which, slot, visible):
        scores = lax.dot_general(
            queries[which], pairs[slot, :, 0:256], (((1,), (1,)), ((), ())),
            preferred_element_type=F32,
        )
        scores = jnp.where(visible, scores, -jnp.inf)
        before = best[which]
        newest = jnp.maximum(before, jnp.max(scores, axis=-1, keepdims=True))
        rescale = jnp.exp(before - newest)
        weights = jnp.exp(scores - jnp.concatenate([newest, newest], axis=1)).astype(BF16)
        total[which] = total[which] * rescale + jnp.sum(
            weights.astype(F32), axis=-1, keepdims=True
        )
        acc[which] = acc[which] * jnp.concatenate([rescale, rescale], axis=1) + jnp.dot(
            weights, pairs[slot, :, 256:512], preferred_element_type=F32
        )
        best[which] = newest

    def visit(slot):
        bound = jnp.where(slot == 0, length, 0)

        def one(which, carry):
            attend(which, slot, k_place >= bound)
            return carry

        lax.fori_loop(
            jnp.where(slot < local, 0, 1), jnp.where(is_helper, 2, 1), one, 0
        )

    own_bound = jnp.where(local == 0, length, 0)
    causal = k_place <= q_place
    attend(0, local, causal & ((k_place >= own_bound) == (q_place >= own_bound)))

    def here(slot):
        pair_copy(0, slot, up).wait_recv()

    @pl.when(is_helper)
    def _():
        ask.wait_recv()
        show.wait_recv()
        attend(1, GROUP, causal)
        visit(local)

    @pl.when(ctx < 63)
    def _():
        tail.wait_recv()

    @pl.when(ctx == 63)
    def _():
        every[256:384, :] = jnp.zeros((PAGE, 512), BF16)

    shifts = [0] * 5
    counts = [0] * 5
    start = 0
    token = ctx * ROWS
    for prompt in range(3):
        size = lengths[prompt]
        head = jnp.maximum(token - start + PAGE - 1, 0) // PAGE
        for number in range(2):
            page = head + number
            row = start + page * PAGE - token
            valid = (row < ROWS) & (page * PAGE < size)
            entry = pages[prompt, jnp.minimum(page, 63)] % 5
            for slot in range(5):
                hit = valid & (entry == slot)
                shifts[slot] = shifts[slot] + jnp.where(hit, row, 0)
                counts[slot] = counts[slot] + jnp.where(hit, jnp.minimum(size - page * PAGE, PAGE), 0)
        start = start + size
    to_row = lax.broadcasted_iota(jnp.int32, (PAGE, 384), 0)
    from_row = lax.broadcasted_iota(jnp.int32, (PAGE, 384), 1)
    for slot in range(5):
        placing = (from_row == to_row + shifts[slot]) & (to_row < counts[slot])
        placing = jnp.where(placing, 1.0, 0.0).astype(BF16)
        cache[slot] = jnp.dot(placing, every[...], preferred_element_type=F32).astype(BF16)

    here(local + 1 - 2 * core)
    visit(local + 1 - 2 * core)

    def event(step, carry):
        crossing = among(step, CROSS)
        row = jnp.where(crossing, 0, z)
        spot = row * 16 + ((y + pick(step, OFFSETS) + 8) % 8) * 2

        @pl.when((z == 1) | jnp.logical_not(crossing))
        def _():
            slot = spot + core
            here(slot)

            @pl.when(goes_up(step))
            def _():
                pair_copy(0, slot, up).start()

            @pl.when(goes_down(step))
            def _():
                pair_copy(1, slot, down).start()

            @pl.when(goes_across(step))
            def _():
                pair_copy(2, slot, across).start()

            pair_copy(3, slot, twin).start()
            visit(slot)
            beside = spot + 1 - core
            here(beside)
            visit(beside)

        return carry

    def goes_up(step):
        return among(step, (1, 4, 10, 13)) | ((step == 8) & (z == 0))

    def goes_down(step):
        return among(step, (2, 5, 11)) | ((step == 9) & (z == 1))

    def goes_across(step):
        return among(step, (1, 2, 4, 5)) & (z == 0)

    lax.fori_loop(1, 16, event, 0)

    @pl.when(is_helper)
    def _():
        helped[0] = (acc[1] / jnp.concatenate([total[1], total[1]], axis=1)).astype(BF16)
        give.start()

    result = (acc[0] / jnp.concatenate([total[0], total[0]], axis=1)).astype(BF16)
    attended[...] = result

    @pl.when(is_helped)
    def _():
        give.wait_recv()
        rows = lax.broadcasted_iota(jnp.int32, (ROWS, 256), 0)
        merged = jnp.where(rows < length, helped[1].astype(F32), attended[...].astype(F32))
        attended[...] = merged.astype(BF16)

    copies_in[5].wait()

    @pl.loop(0, 8)
    def _(b):
        cols = pl.ds(pl.multiple_of(b * 256, 256), 256)
        terms[b] = jnp.dot(
            attended[...], w_out_v[:, cols], preferred_element_type=F32
        ).astype(BF16)

    def sum_copy(number, src, dst, peer):
        return remote(src, dst, rs_send.at[number], rs_recv.at[number], tp=peer)

    first_ups, first_downs = [], []
    for k in range(2):
        side = (1 - half if k == 0 else half) * 4
        far = side + (x + 2) % 4
        first_ups.append(sum_copy(4 * k, terms.at[far, top], first.at[k, top], x_up))
        first_downs.append(
            sum_copy(4 * k + 1, terms.at[far, bottom], first.at[k, bottom], x_down)
        )
        first_ups[k].start()
        first_downs[k].start()
    seconds = []
    for k in range(2):
        side = (1 - half if k == 0 else half) * 4
        to_up, to_down = side + (x + 1) % 4, side + (x + 3) % 4
        first_ups[k].wait_recv()
        terms[to_up, top] = (
            terms[to_up, top].astype(F32) + first[k, top].astype(F32)
        ).astype(BF16)
        one = sum_copy(4 * k + 2, terms.at[to_up], second.at[k, 0], x_up)
        one.start()
        first_downs[k].wait_recv()
        terms[to_down, bottom] = (
            terms[to_down, bottom].astype(F32) + first[k, bottom].astype(F32)
        ).astype(BF16)
        two = sum_copy(4 * k + 3, terms.at[to_down], second.at[k, 1], x_down)
        two.start()
        seconds.append((one, two))

    def summed(k):
        side = (1 - half if k == 0 else half) * 4
        for copy in seconds[k]:
            copy.wait_recv()
        return (
            terms[side + x].astype(F32) + second[k, 0].astype(F32) + second[k, 1].astype(F32)
        )

    last[0] = summed(0).astype(BF16)
    final = sum_copy(8, last.at[0], last.at[1], mirror)
    final.start()
    kept = summed(1)
    final.wait_recv()
    out[...] = (kept + last[1].astype(F32)).astype(BF16)

    for copy in first_ups + first_downs + [c for pair in seconds for c in pair] + [final]:
        copy.wait_send()

    @pl.when(ctx > 0)
    def _():
        tail.wait_send()

    @pl.when(is_helped)
    def _():
        ask.wait_send()
        show.wait_send()

    @pl.when(is_helper)
    def _():
        give.wait_send()

    pair_copy(0, local, up).wait_send()
    pair_copy(1, local, down).wait_send()

    @pl.when(z == 0)
    def _():
        pair_copy(2, local, across).wait_send()

    pair_copy(3, local, twin).wait_send()

    def drain(step, carry):
        crossing = among(step, CROSS)
        row = jnp.where(crossing, 0, z)
        slot = row * 16 + ((y + pick(step, OFFSETS) + 8) % 8) * 2 + core

        @pl.when((z == 1) | jnp.logical_not(crossing))
        def _():
            @pl.when(goes_up(step))
            def _():
                pair_copy(0, slot, up).wait_send()

            @pl.when(goes_down(step))
            def _():
                pair_copy(1, slot, down).wait_send()

            @pl.when(goes_across(step))
            def _():
                pair_copy(2, slot, across).wait_send()

            pair_copy(3, slot, twin).wait_send()

        return carry

    lax.fori_loop(1, 16, drain, 0)


def per_device(hidden_in, ln_gain, ln_bias, w_qkv, w_out, segment_ids, prompt_lengths, page_table):
    inverse = np.float32(10000.0) ** -(np.arange(0, 64, 2, dtype=np.float32) / np.float32(64))
    inverse = np.tile(inverse.astype(np.float32), 4)[None, :]
    vmem = pl.BlockSpec(memory_space=pltpu.VMEM)
    smem = pl.BlockSpec(memory_space=pltpu.SMEM)
    held = pl.BlockSpec(memory_space=pl.ANY)
    dma = pltpu.SemaphoreType.DMA
    attn_out, cache = pl.pallas_call(
        kernel,
        out_shape=(
            jax.ShapeDtypeStruct((ROWS, 256), BF16),
            jax.ShapeDtypeStruct((5, PAGE, 512), BF16),
        ),
        in_specs=[smem, smem] + [held] * 6,
        out_specs=(vmem, vmem),
        scratch_shapes=[
            pltpu.VMEM((ROWS, 256), BF16),
            pltpu.VMEM((1, 2048), F32),
            pltpu.VMEM((1, 2048), F32),
            pltpu.VMEM((1, 128), F32),
            pltpu.VMEM((ROWS, 128), F32),
            pltpu.VMEM((ROWS, 128), F32),
            pltpu.VMEM((8, ROWS, 256), BF16),
            pltpu.VMEM((ROWS, 2048), BF16),
            pltpu.VMEM((3, 2048, 256), BF16),
            pltpu.VMEM((256, 2048), BF16),
            pltpu.VMEM((2, ROWS, 256), BF16),
            pltpu.VMEM((GROUP + 1, ROWS, 512), BF16),
            pltpu.VMEM((384, 512), BF16),
            pltpu.VMEM((2, ROWS, 128), F32),
            pltpu.VMEM((2, ROWS, 128), F32),
            pltpu.VMEM((2, ROWS, 256), F32),
            pltpu.VMEM((2, ROWS, 256), BF16),
            pltpu.VMEM((ROWS, 256), BF16),
            pltpu.VMEM((8, ROWS, 256), BF16),
            pltpu.VMEM((2, ROWS, 256), BF16),
            pltpu.VMEM((2, 2, ROWS, 256), BF16),
            pltpu.VMEM((2, ROWS, 256), BF16),
            dma((6,)),
            dma((9,)),
            dma((8, 2)),
            dma((4, GROUP)),
            dma((GROUP,)),
            dma((4,)),
            dma((4,)),
            dma((9,)),
            dma((9,)),
        ],
        compiler_params=pltpu.CompilerParams(
            collective_id=0, has_side_effects=True, vmem_limit_bytes=62 * 1024 * 1024
        ),
    )(
        prompt_lengths, page_table, hidden_in, ln_gain.reshape(1, -1), ln_bias.reshape(1, -1),
        jnp.asarray(inverse), w_qkv, w_out,
    )
    return (attn_out, cache.reshape(5, PAGE, 2, 256))


def solution(mesh):
    return jax.shard_map(
        per_device,
        mesh=mesh,
        in_specs=(P("ctx", "tp"), P(), P(), P(None, None, "tp"), P("tp", None), P("ctx"), P(), P()),
        out_specs=(P("ctx", "tp"), P("ctx", None, None, "tp")),
        check_vma=False,
    )
```

```python
import jax
import numpy as np
import jax.numpy as jnp
from jax import lax
from jax.experimental import pallas as pl
from jax.experimental.pallas import tpu as pltpu
from jax.sharding import PartitionSpec as P

HD = 256
PAGE = 128
ROWS = 256
GROUP = 32
EPSILON = 1e-05
TURN = (6.28125, 0.00193500518798828125, 3.0197e-07)
MESH = pl.DeviceIdType.MESH
F32 = jnp.float32
BF16 = jnp.bfloat16

OFFSETS = (0, -1, 1, -2, 2, -3, 3)


def pick(step, table):
    value = 0
    for place, entry in enumerate(table):
        if entry != 0:
            value = value + jnp.where(step == place, entry, 0)
    return value


def remote(src, dst, send, recv, **where):
    return pltpu.make_async_remote_copy(
        src_ref=src, dst_ref=dst, send_sem=send, recv_sem=recv, device_id=where, device_id_type=MESH
    )


def kernel(
    lengths, pages, hidden_h, gain_h, bias_h, inverse_h, w_qkv, w_out,
    out, cache,
    hidden, gain, bias, inverse, cosine, sine, gathered, normed, w_qkv_v, w_out_v, queries, pairs, every, best, total, acc,
    reply, weight, attended, terms, first, second, last,
    local_sem, ag_send, ag_recv, kv_send, kv_recv, far_send, far_recv, extra_send, extra_recv, rs_send, rs_recv,
):
    ctx = lax.axis_index("ctx")
    tp = lax.axis_index("tp")
    group = ctx // GROUP
    local = ctx % GROUP
    z = local // 16
    y = (local // 2) % 8
    core = local % 2
    base = group * GROUP
    half = tp // 4
    x = tp % 4
    up = base + z * 16 + ((y + 1) % 8) * 2 + core
    down = base + z * 16 + ((y + 7) % 8) * 2 + core
    twin = base + z * 16 + y * 2 + (1 - core)
    across = base + (1 - z) * 16 + y * 2 + core
    x_up = half * 4 + (x + 1) % 4
    x_down = half * 4 + (x + 3) % 4
    x_far = half * 4 + (x + 2) % 4
    mirror = (1 - half) * 4 + x
    place = local % 16
    is_helper = (ctx == 0) | (ctx == 16)
    is_helped = ctx == 32

    copies_in = [
        pltpu.make_async_copy(source, target, local_sem.at[number])
        for number, (source, target) in enumerate((
            (hidden_h, hidden), (inverse_h, inverse), (gain_h, gain), (bias_h, bias),
            (w_qkv, w_qkv_v), (w_out, w_out_v),
        ))
    ]
    for copy in copies_in:
        copy.start()

    barrier = pltpu.get_barrier_semaphore()
    for peer in (up, down, twin, across):
        pl.semaphore_signal(barrier, inc=1, device_id={"ctx": peer}, device_id_type=MESH)
    for peer in (x_up, x_down, mirror):
        pl.semaphore_signal(barrier, inc=1, device_id={"tp": peer}, device_id_type=MESH)

    @pl.when(ctx > 0)
    def _():
        pl.semaphore_signal(barrier, inc=1, device_id={"ctx": ctx - 1}, device_id_type=MESH)

    @pl.when(ctx < 63)
    def _():
        pl.semaphore_signal(barrier, inc=1, device_id={"ctx": ctx + 1}, device_id_type=MESH)

    @pl.when(is_helper)
    def _():
        pl.semaphore_signal(barrier, inc=1, device_id={"ctx": 32}, device_id_type=MESH)

    @pl.when(is_helped)
    def _():
        for peer in (0, 16):
            pl.semaphore_signal(barrier, inc=1, device_id={"ctx": peer}, device_id_type=MESH)

    pl.semaphore_wait(
        barrier,
        7 + jnp.where(ctx > 0, 1, 0) + jnp.where(ctx < 63, 1, 0)
        + jnp.where(is_helper, 1, 0) + jnp.where(is_helped, 2, 0),
    )

    top, bottom = pl.ds(0, 128), pl.ds(128, 128)

    def feature_copy(number, src, slot, part, peer, rows=None):
        dst = gathered.at[slot] if rows is None else gathered.at[slot, rows]
        return remote(src, dst, ag_send.at[number], ag_recv.at[slot, part], tp=peer)

    copies_in[0].wait()
    own_z = feature_copy(0, hidden, tp, 0, mirror)
    own_up = feature_copy(1, hidden, tp, 0, x_up)
    own_down = feature_copy(2, hidden, tp, 0, x_down)
    for copy in (own_z, own_up, own_down):
        copy.start()
    gathered[tp] = hidden[...]
    sent = [own_z, own_up, own_down]

    copies_in[1].wait()
    index = ctx * ROWS + lax.broadcasted_iota(jnp.int32, (ROWS, 128), 0)
    lane = lax.broadcasted_iota(jnp.int32, (ROWS, 128), 1)
    length = lengths[0]
    both = length + lengths[1]
    places = index - jnp.where(index < length, 0, jnp.where(index < both, length, both))
    angles = places.astype(F32) * inverse[...]
    turns = jnp.floor(angles * F32(0.15915494309189535) + 0.5)
    for part in TURN:
        angles = angles - turns * F32(part)
    cosine[...] = jnp.where(lane < 64, jnp.cos(angles), 1.0)
    sine[...] = jnp.where(
        lane < 32, -jnp.sin(angles), jnp.where(lane < 64, jnp.sin(angles), 0.0)
    )

    def arrived(slot, part, rows=None):
        dst = gathered.at[slot] if rows is None else gathered.at[slot, rows]
        remote(dst, dst, ag_send.at[0], ag_recv.at[slot, part], tp=mirror).wait_recv()

    def pass_on(slot_down, slot_up, number):
        arrived(slot_down, 0)
        one = feature_copy(number, gathered.at[slot_down, top], slot_down, 0, x_up, top)
        one.start()
        arrived(slot_up, 0)
        two = feature_copy(number + 1, gathered.at[slot_up, bottom], slot_up, 1, x_down, bottom)
        two.start()
        sent.extend([one, two])

    pass_on(x_down, x_up, 3)
    other = (1 - half) * 4
    arrived(mirror, 0)
    cross_up = feature_copy(5, gathered.at[mirror], mirror, 0, x_up)
    cross_down = feature_copy(6, gathered.at[mirror], mirror, 0, x_down)
    cross_up.start()
    cross_down.start()
    sent.extend([cross_up, cross_down])
    arrived(x_far, 0, top)
    arrived(x_far, 1, bottom)
    pass_on(other + (x + 3) % 4, other + (x + 1) % 4, 7)
    arrived(other + (x + 2) % 4, 0, top)
    arrived(other + (x + 2) % 4, 1, bottom)
    for copy in sent:
        copy.wait_send()

    copies_in[2].wait()
    copies_in[3].wait()
    @pl.loop(0, ROWS // 32)
    def _(step):
        rows = pl.ds(pl.multiple_of(step * 32, 32), 32)
        blocks = [gathered[b, rows, :].astype(F32) for b in range(8)]
        average = jnp.sum(sum(blocks), axis=-1, keepdims=True) / 2048
        centered = [block - average for block in blocks]
        spread = jnp.sum(sum(c * c for c in centered), axis=-1, keepdims=True) / 2048
        scale = lax.rsqrt(spread + EPSILON)
        for b in range(8):
            cols = pl.ds(b * 256, 256)
            value = centered[b] * scale * gain[:, cols] + bias[:, cols]
            normed[rows, cols] = value.astype(BF16)

    copies_in[4].wait()

    def turn(value):
        lead = value[:, :128]
        turned = jnp.where(lane < 32, pltpu.roll(lead, 96, 1), pltpu.roll(lead, 32, 1))
        lead = lead * cosine[...] + turned * sine[...]
        return jnp.concatenate([lead, value[:, 128:]], axis=1).astype(BF16)

    key = turn(jnp.dot(normed[...], w_qkv_v[1], preferred_element_type=F32))
    pairs[place, :, 0:256] = key
    every[0:256, 0:256] = key
    value = jnp.dot(normed[...], w_qkv_v[2], preferred_element_type=F32).astype(BF16)
    pairs[place, :, 256:512] = value
    every[0:256, 256:512] = value

    def pair_copy(way, slot, peer):
        return remote(
            pairs.at[slot], pairs.at[slot], kv_send.at[way, slot], kv_recv.at[slot], ctx=peer
        )

    pair_copy(0, place, up).start()
    pair_copy(1, place, down).start()
    pair_copy(2, place, twin).start()
    tail = remote(
        pairs.at[place, pl.ds(0, PAGE)], every.at[pl.ds(256, PAGE)],
        extra_send.at[0], extra_recv.at[0], ctx=jnp.maximum(ctx - 1, 0),
    )

    @pl.when(ctx > 0)
    def _():
        tail.start()

    query = turn(jnp.dot(normed[...], w_qkv_v[0], preferred_element_type=F32))
    queries[0] = query * jnp.asarray(1 / 16, BF16)

    def message(src, dst, number, peer):
        return remote(src, dst, extra_send.at[number], extra_recv.at[number], ctx=peer)

    ask = message(queries.at[0], queries.at[1], 1, across)
    asks = [message(queries.at[0], queries.at[2], 2 + i, 16 * i) for i in range(2)]
    show = message(pairs.at[place], pairs.at[16], 4, 16)
    gives = [
        message(reply.at[0], reply.at[2], 5, across),
        message(weight.at[0], weight.at[2], 6, across),
    ]
    back = 7 + 2 * z
    helps = [
        remote(reply.at[1], reply.at[3 + z], extra_send.at[7], extra_recv.at[back], ctx=32),
        remote(weight.at[1], weight.at[3 + z], extra_send.at[8], extra_recv.at[back + 1], ctx=32),
    ]

    @pl.when(z == 1)
    def _():
        ask.start()

    @pl.when(is_helped)
    def _():
        asks[1].start()
        show.start()
        asks[0].start()

    best[...] = jnp.full(best.shape, -jnp.inf, F32)
    total[...] = jnp.zeros(total.shape, F32)
    acc[...] = jnp.zeros(acc.shape, F32)
    q_place = lax.broadcasted_iota(jnp.int32, (ROWS, ROWS), 0)
    k_place = lax.broadcasted_iota(jnp.int32, (ROWS, ROWS), 1)

    def attend(which, slot, visible):
        scores = lax.dot_general(
            queries[which], pairs[slot, :, 0:256], (((1,), (1,)), ((), ())),
            preferred_element_type=F32,
        )
        scores = jnp.where(visible, scores, -jnp.inf)
        before = best[which]
        newest = jnp.maximum(before, jnp.max(scores, axis=-1, keepdims=True))
        rescale = jnp.exp(before - newest)
        weights = jnp.exp(scores - jnp.concatenate([newest, newest], axis=1)).astype(BF16)
        total[which] = total[which] * rescale + jnp.sum(
            weights.astype(F32), axis=-1, keepdims=True
        )
        acc[which] = acc[which] * jnp.concatenate([rescale, rescale], axis=1) + jnp.dot(
            weights, pairs[slot, :, 256:512], preferred_element_type=F32
        )
        best[which] = newest

    def visit(slot):
        bound = jnp.where((slot == 0) & (z == 0), length, 0)

        def one(which, carry):
            @pl.when(
                ((which == 0) & (slot < place))
                | ((which == 1) & (z == 0))
                | ((which == 2) & is_helper)
            )
            def _():
                attend(which, slot, k_place >= bound)

            return carry

        lax.fori_loop(0, 3, one, 0)

    own_bound = jnp.where(local == 0, length, 0)
    causal = k_place <= q_place
    attend(0, place, causal & ((k_place >= own_bound) == (q_place >= own_bound)))

    def here(slot):
        pair_copy(0, slot, up).wait_recv()

    @pl.when(ctx < 63)
    def _():
        tail.wait_recv()

    @pl.when(ctx == 63)
    def _():
        every[256:384, :] = jnp.zeros((PAGE, 512), BF16)

    shifts = [0] * 5
    counts = [0] * 5
    start = 0
    token = ctx * ROWS
    for prompt in range(3):
        size = lengths[prompt]
        head = jnp.maximum(token - start + PAGE - 1, 0) // PAGE
        for number in range(2):
            page = head + number
            row = start + page * PAGE - token
            valid = (row < ROWS) & (page * PAGE < size)
            entry = pages[prompt, jnp.minimum(page, 63)] % 5
            for slot in range(5):
                hit = valid & (entry == slot)
                shifts[slot] = shifts[slot] + jnp.where(hit, row, 0)
                counts[slot] = counts[slot] + jnp.where(hit, jnp.minimum(size - page * PAGE, PAGE), 0)
        start = start + size
    to_row = lax.broadcasted_iota(jnp.int32, (PAGE, 384), 0)
    from_row = lax.broadcasted_iota(jnp.int32, (PAGE, 384), 1)
    for slot in range(5):
        placing = (from_row == to_row + shifts[slot]) & (to_row < counts[slot])
        placing = jnp.where(placing, 1.0, 0.0).astype(BF16)
        cache[slot] = jnp.dot(placing, every[...], preferred_element_type=F32).astype(BF16)

    @pl.when(z == 0)
    def _():
        ask.wait_recv()

    @pl.when(ctx == 0)
    def _():
        asks[0].wait_recv()

    @pl.when(ctx == 16)
    def _():
        asks[1].wait_recv()
        show.wait_recv()
        attend(2, 16, causal)

    visit(place)
    here(place + 1 - 2 * core)
    visit(place + 1 - 2 * core)

    def spot(step):
        return ((y + pick(step, OFFSETS) + 8) % 8) * 2

    def event(step, carry):
        slot = spot(step) + core
        here(slot)

        @pl.when((step == 1) | (step == 3))
        def _():
            pair_copy(0, slot, up).start()

        @pl.when((step == 2) | (step == 4))
        def _():
            pair_copy(1, slot, down).start()

        @pl.when(step == 5)
        def _():
            half_copy(0, slot, up).start()

        @pl.when(step == 6)
        def _():
            half_copy(1, slot, down).start()

        pair_copy(2, slot, twin).start()
        visit(slot)
        beside = spot(step) + 1 - core
        here(beside)
        visit(beside)
        return carry

    def half_copy(way, slot, peer):
        rows = pl.ds(way * 128, 128)
        return remote(
            pairs.at[slot, rows], pairs.at[slot, rows],
            far_send.at[way], far_recv.at[way], ctx=peer,
        )

    lax.fori_loop(1, 7, event, 0)
    opposite = ((y + 4) % 8) * 2
    half_copy(0, opposite + core, up).wait_recv()
    half_copy(1, opposite + core, down).wait_recv()
    pair_copy(2, opposite + core, twin).start()
    visit(opposite + core)
    here(opposite + 1 - core)
    visit(opposite + 1 - core)

    def wide(value):
        return jnp.concatenate([value, value], axis=1)

    def hand_back(which, copies):
        reply[which - 1] = (acc[which] / wide(total[which])).astype(BF16)
        weight[which - 1] = jnp.transpose(best[which] + jnp.log(total[which]))[0:8]
        for copy in copies:
            copy.start()

    @pl.when(z == 0)
    def _():
        hand_back(1, gives)

    @pl.when(is_helper)
    def _():
        hand_back(2, helps)

    def logs(number):
        return jnp.transpose(jnp.tile(weight[number], (16, 1)))

    result = acc[0] / wide(total[0])
    attended[...] = result.astype(BF16)

    def blend(one, one_log, two, two_log):
        most = jnp.maximum(one_log, two_log)
        one_part, two_part = jnp.exp(one_log - most), jnp.exp(two_log - most)
        share = one_part / (one_part + two_part)
        other_share = two_part / (one_part + two_part)
        return one * wide(share) + two * wide(other_share)

    @pl.when(z == 1)
    def _():
        for copy in gives:
            copy.wait_recv()
        mixed = blend(
            acc[0] / wide(total[0]), best[0] + jnp.log(total[0]), reply[2].astype(F32), logs(2)
        )
        attended[...] = mixed.astype(BF16)

    @pl.when(is_helped)
    def _():
        for number in range(2):
            remote(
                reply.at[1], reply.at[3 + number],
                extra_send.at[7], extra_recv.at[7 + 2 * number], ctx=0,
            ).wait_recv()
            remote(
                weight.at[1], weight.at[3 + number],
                extra_send.at[8], extra_recv.at[8 + 2 * number], ctx=0,
            ).wait_recv()
        mixed = blend(reply[3].astype(F32), logs(3), reply[4].astype(F32), logs(4))
        rows = lax.broadcasted_iota(jnp.int32, (ROWS, 256), 0)
        attended[...] = jnp.where(
            rows < length, mixed, attended[...].astype(F32)
        ).astype(BF16)

    copies_in[5].wait()

    @pl.loop(0, 8)
    def _(b):
        cols = pl.ds(pl.multiple_of(b * 256, 256), 256)
        terms[b] = jnp.dot(
            attended[...], w_out_v[:, cols], preferred_element_type=F32
        ).astype(BF16)

    def sum_copy(number, src, dst, peer):
        return remote(src, dst, rs_send.at[number], rs_recv.at[number], tp=peer)

    first_ups, first_downs = [], []
    for k in range(2):
        side = (1 - half if k == 0 else half) * 4
        far = side + (x + 2) % 4
        first_ups.append(sum_copy(4 * k, terms.at[far, top], first.at[k, top], x_up))
        first_downs.append(
            sum_copy(4 * k + 1, terms.at[far, bottom], first.at[k, bottom], x_down)
        )
        first_ups[k].start()
        first_downs[k].start()
    seconds = []
    for k in range(2):
        side = (1 - half if k == 0 else half) * 4
        to_up, to_down = side + (x + 1) % 4, side + (x + 3) % 4
        first_ups[k].wait_recv()
        terms[to_up, top] = (
            terms[to_up, top].astype(F32) + first[k, top].astype(F32)
        ).astype(BF16)
        one = sum_copy(4 * k + 2, terms.at[to_up], second.at[k, 0], x_up)
        one.start()
        first_downs[k].wait_recv()
        terms[to_down, bottom] = (
            terms[to_down, bottom].astype(F32) + first[k, bottom].astype(F32)
        ).astype(BF16)
        two = sum_copy(4 * k + 3, terms.at[to_down], second.at[k, 1], x_down)
        two.start()
        seconds.append((one, two))

    def summed(k):
        side = (1 - half if k == 0 else half) * 4
        for copy in seconds[k]:
            copy.wait_recv()
        return (
            terms[side + x].astype(F32) + second[k, 0].astype(F32) + second[k, 1].astype(F32)
        )

    last[0] = summed(0).astype(BF16)
    final = sum_copy(8, last.at[0], last.at[1], mirror)
    final.start()
    kept = summed(1)
    final.wait_recv()
    out[...] = (kept + last[1].astype(F32)).astype(BF16)

    for copy in first_ups + first_downs + [c for pair in seconds for c in pair] + [final]:
        copy.wait_send()

    @pl.when(ctx > 0)
    def _():
        tail.wait_send()

    @pl.when(z == 1)
    def _():
        ask.wait_send()

    @pl.when(is_helped)
    def _():
        for copy in asks + [show]:
            copy.wait_send()

    @pl.when(z == 0)
    def _():
        for copy in gives:
            copy.wait_send()

    @pl.when(is_helper)
    def _():
        for copy in helps:
            copy.wait_send()

    pair_copy(0, place, up).wait_send()
    pair_copy(1, place, down).wait_send()
    pair_copy(2, place, twin).wait_send()
    for step in range(1, 7):
        slot = spot(step) + core
        if step in (1, 3):
            pair_copy(0, slot, up).wait_send()
        if step in (2, 4):
            pair_copy(1, slot, down).wait_send()
        if step in (5, 6):
            half_copy(step - 5, slot, up).wait_send()
        pair_copy(2, slot, twin).wait_send()
    pair_copy(2, opposite + core, twin).wait_send()


def per_device(hidden_in, ln_gain, ln_bias, w_qkv, w_out, segment_ids, prompt_lengths, page_table):
    inverse = np.float32(10000.0) ** -(np.arange(0, 64, 2, dtype=np.float32) / np.float32(64))
    inverse = np.tile(inverse.astype(np.float32), 4)[None, :]
    vmem = pl.BlockSpec(memory_space=pltpu.VMEM)
    smem = pl.BlockSpec(memory_space=pltpu.SMEM)
    held = pl.BlockSpec(memory_space=pl.ANY)
    dma = pltpu.SemaphoreType.DMA
    attn_out, cache = pl.pallas_call(
        kernel,
        out_shape=(
            jax.ShapeDtypeStruct((ROWS, 256), BF16),
            jax.ShapeDtypeStruct((5, PAGE, 512), BF16),
        ),
        in_specs=[smem, smem] + [held] * 6,
        out_specs=(vmem, vmem),
        scratch_shapes=[
            pltpu.VMEM((ROWS, 256), BF16),
            pltpu.VMEM((1, 2048), F32),
            pltpu.VMEM((1, 2048), F32),
            pltpu.VMEM((1, 128), F32),
            pltpu.VMEM((ROWS, 128), F32),
            pltpu.VMEM((ROWS, 128), F32),
            pltpu.VMEM((8, ROWS, 256), BF16),
            pltpu.VMEM((ROWS, 2048), BF16),
            pltpu.VMEM((3, 2048, 256), BF16),
            pltpu.VMEM((256, 2048), BF16),
            pltpu.VMEM((3, ROWS, 256), BF16),
            pltpu.VMEM((17, ROWS, 512), BF16),
            pltpu.VMEM((384, 512), BF16),
            pltpu.VMEM((3, ROWS, 128), F32),
            pltpu.VMEM((3, ROWS, 128), F32),
            pltpu.VMEM((3, ROWS, 256), F32),
            pltpu.VMEM((5, ROWS, 256), BF16),
            pltpu.VMEM((5, 8, 256), F32),
            pltpu.VMEM((ROWS, 256), BF16),
            pltpu.VMEM((8, ROWS, 256), BF16),
            pltpu.VMEM((2, ROWS, 256), BF16),
            pltpu.VMEM((2, 2, ROWS, 256), BF16),
            pltpu.VMEM((2, ROWS, 256), BF16),
            dma((6,)),
            dma((9,)),
            dma((8, 2)),
            dma((3, 16)),
            dma((16,)),
            dma((2,)),
            dma((2,)),
            dma((11,)),
            dma((11,)),
            dma((9,)),
            dma((9,)),
        ],
        compiler_params=pltpu.CompilerParams(
            collective_id=0, has_side_effects=True, vmem_limit_bytes=62 * 1024 * 1024
        ),
    )(
        prompt_lengths, page_table, hidden_in, ln_gain.reshape(1, -1), ln_bias.reshape(1, -1),
        jnp.asarray(inverse), w_qkv, w_out,
    )
    return (attn_out, cache.reshape(5, PAGE, 2, 256))


def solution(mesh):
    return jax.shard_map(
        per_device,
        mesh=mesh,
        in_specs=(P("ctx", "tp"), P(), P(), P(None, None, "tp"), P("tp", None), P("ctx"), P(), P()),
        out_specs=(P("ctx", "tp"), P("ctx", None, None, "tp")),
        check_vma=False,
    )
```

```python
import jax
import numpy as np
import jax.numpy as jnp
from jax import lax
from jax.experimental import pallas as pl
from jax.experimental.pallas import tpu as pltpu
from jax.sharding import PartitionSpec as P

HD = 256
PAGE = 128
ROWS = 256
GROUP = 32
EPSILON = 1e-05
TURN = (6.28125, 0.00193500518798828125, 3.0197e-07)
MESH = pl.DeviceIdType.MESH
F32 = jnp.float32
BF16 = jnp.bfloat16

OFFSETS = (0, -1, 1, -2, 2, -3, 3)


def pick(step, table):
    value = 0
    for place, entry in enumerate(table):
        if entry != 0:
            value = value + jnp.where(step == place, entry, 0)
    return value


def remote(src, dst, send, recv, **where):
    return pltpu.make_async_remote_copy(
        src_ref=src, dst_ref=dst, send_sem=send, recv_sem=recv, device_id=where, device_id_type=MESH
    )


def kernel(
    lengths, pages, hidden_h, gain_h, bias_h, inverse_h, w_qkv, w_out,
    out, cache,
    hidden, gain, bias, inverse, cosine, sine, gathered, normed, w_qkv_v, w_out_v, queries, pairs, every, best, total, acc,
    reply, weight, attended, terms, first, second, last,
    relay, relay_recv, local_sem, ag_send, ag_recv, kv_send, kv_recv, far_send, far_recv, extra_send, extra_recv, rs_send, rs_recv,
):
    ctx = lax.axis_index("ctx")
    tp = lax.axis_index("tp")
    group = ctx // GROUP
    local = ctx % GROUP
    z = local // 16
    y = (local // 2) % 8
    core = local % 2
    base = group * GROUP
    half = tp // 4
    x = tp % 4
    up = base + z * 16 + ((y + 1) % 8) * 2 + core
    down = base + z * 16 + ((y + 7) % 8) * 2 + core
    twin = base + z * 16 + y * 2 + (1 - core)
    across = base + (1 - z) * 16 + y * 2 + core
    x_up = half * 4 + (x + 1) % 4
    x_down = half * 4 + (x + 3) % 4
    x_far = half * 4 + (x + 2) % 4
    mirror = (1 - half) * 4 + x
    place = local % 16
    is_helper = (ctx == 0) | (ctx == 16)
    is_helped = ctx == 32

    def along_z(steps):
        there = (half * 4 + ctx // 16 + steps) % 8
        return {"ctx": (there % 4) * 16 + ctx % 16, "tp": (there // 4) * 4 + x}


    copies_in = [
        pltpu.make_async_copy(source, target, local_sem.at[number])
        for number, (source, target) in enumerate((
            (hidden_h, hidden), (inverse_h, inverse), (gain_h, gain), (bias_h, bias),
            (w_qkv, w_qkv_v), (w_out, w_out_v),
        ))
    ]
    for copy in copies_in:
        copy.start()

    barrier = pltpu.get_barrier_semaphore()
    for peer in (up, down, twin, across):
        pl.semaphore_signal(barrier, inc=1, device_id={"ctx": peer}, device_id_type=MESH)
    for peer in (x_up, x_down, mirror):
        pl.semaphore_signal(barrier, inc=1, device_id={"tp": peer}, device_id_type=MESH)

    for steps in (1, 3, 5, 7):
        pl.semaphore_signal(barrier, inc=1, device_id=along_z(steps), device_id_type=MESH)

    @pl.when(ctx > 0)
    def _():
        pl.semaphore_signal(barrier, inc=1, device_id={"ctx": ctx - 1}, device_id_type=MESH)

    @pl.when(ctx < 63)
    def _():
        pl.semaphore_signal(barrier, inc=1, device_id={"ctx": ctx + 1}, device_id_type=MESH)

    @pl.when(is_helper)
    def _():
        pl.semaphore_signal(barrier, inc=1, device_id={"ctx": 32}, device_id_type=MESH)

    @pl.when(is_helped)
    def _():
        for peer in (0, 16):
            pl.semaphore_signal(barrier, inc=1, device_id={"ctx": peer}, device_id_type=MESH)

    pl.semaphore_wait(
        barrier,
        11 + jnp.where(ctx > 0, 1, 0) + jnp.where(ctx < 63, 1, 0)
        + jnp.where(is_helper, 1, 0) + jnp.where(is_helped, 2, 0),
    )

    top, bottom = pl.ds(0, 128), pl.ds(128, 128)

    def feature_copy(number, src, slot, part, peer, rows=None):
        dst = gathered.at[slot] if rows is None else gathered.at[slot, rows]
        return remote(src, dst, ag_send.at[number], ag_recv.at[slot, part], tp=peer)

    copies_in[0].wait()
    own_z = feature_copy(0, hidden.at[top], tp, 0, mirror, top)
    own_relay = remote(hidden.at[bottom], relay.at[0], ag_send.at[9], relay_recv.at[0], **along_z(7))
    own_up = feature_copy(1, hidden, tp, 0, x_up)
    own_down = feature_copy(2, hidden, tp, 0, x_down)
    for copy in (own_z, own_relay, own_up, own_down):
        copy.start()
    gathered[tp] = hidden[...]
    sent = [own_z, own_relay, own_up, own_down]

    copies_in[1].wait()
    index = ctx * ROWS + lax.broadcasted_iota(jnp.int32, (ROWS, 128), 0)
    lane = lax.broadcasted_iota(jnp.int32, (ROWS, 128), 1)
    length = lengths[0]
    both = length + lengths[1]
    places = index - jnp.where(index < length, 0, jnp.where(index < both, length, both))
    angles = places.astype(F32) * inverse[...]
    turns = jnp.floor(angles * F32(0.15915494309189535) + 0.5)
    for part in TURN:
        angles = angles - turns * F32(part)
    cosine[...] = jnp.where(lane < 64, jnp.cos(angles), 1.0)
    sine[...] = jnp.where(
        lane < 32, -jnp.sin(angles), jnp.where(lane < 64, jnp.sin(angles), 0.0)
    )

    def arrived(slot, part, rows=None):
        dst = gathered.at[slot] if rows is None else gathered.at[slot, rows]
        remote(dst, dst, ag_send.at[0], ag_recv.at[slot, part], tp=mirror).wait_recv()

    def send(copy):
        copy.start()
        sent.append(copy)

    own_relay.wait_recv()
    origin = along_z(1)["tp"]
    send(remote(
        relay.at[0], gathered.at[origin, bottom], ag_send.at[10], ag_recv.at[origin, 1],
        **along_z(5),
    ))

    arrived(x_down, 0)
    send(feature_copy(3, gathered.at[x_down, top], x_down, 0, x_up, top))
    arrived(x_up, 0)
    send(feature_copy(4, gathered.at[x_up, bottom], x_up, 1, x_down, bottom))
    other = (1 - half) * 4
    beyond_down, beyond_up = other + (x + 3) % 4, other + (x + 1) % 4
    beyond_far = other + (x + 2) % 4
    arrived(mirror, 0, top)
    send(feature_copy(5, gathered.at[mirror, top], mirror, 0, x_up, top))
    send(feature_copy(6, gathered.at[mirror, top], mirror, 0, x_down, top))
    arrived(beyond_down, 0, top)
    send(feature_copy(7, gathered.at[beyond_down, top], beyond_down, 0, x_up, top))
    arrived(mirror, 1, bottom)
    send(feature_copy(11, gathered.at[mirror, bottom], mirror, 1, x_up, bottom))
    send(feature_copy(12, gathered.at[mirror, bottom], mirror, 1, x_down, bottom))
    arrived(beyond_up, 1, bottom)
    send(feature_copy(8, gathered.at[beyond_up, bottom], beyond_up, 1, x_down, bottom))
    for slot in (x_far, beyond_far):
        arrived(slot, 0, top)
        arrived(slot, 1, bottom)
    arrived(beyond_down, 1, bottom)
    arrived(beyond_up, 0, top)
    for copy in sent:
        copy.wait_send()

    copies_in[2].wait()
    copies_in[3].wait()
    @pl.loop(0, ROWS // 32)
    def _(step):
        rows = pl.ds(pl.multiple_of(step * 32, 32), 32)
        blocks = [gathered[b, rows, :].astype(F32) for b in range(8)]
        average = jnp.sum(sum(blocks), axis=-1, keepdims=True) / 2048
        centered = [block - average for block in blocks]
        spread = jnp.sum(sum(c * c for c in centered), axis=-1, keepdims=True) / 2048
        scale = lax.rsqrt(spread + EPSILON)
        for b in range(8):
            cols = pl.ds(b * 256, 256)
            value = centered[b] * scale * gain[:, cols] + bias[:, cols]
            normed[rows, cols] = value.astype(BF16)

    copies_in[4].wait()

    def turn(value):
        lead = value[:, :128]
        turned = jnp.where(lane < 32, pltpu.roll(lead, 96, 1), pltpu.roll(lead, 32, 1))
        lead = lead * cosine[...] + turned * sine[...]
        return jnp.concatenate([lead, value[:, 128:]], axis=1).astype(BF16)

    key = turn(jnp.dot(normed[...], w_qkv_v[1], preferred_element_type=F32))
    pairs[place, :, 0:256] = key
    every[0:256, 0:256] = key
    value = jnp.dot(normed[...], w_qkv_v[2], preferred_element_type=F32).astype(BF16)
    pairs[place, :, 256:512] = value
    every[0:256, 256:512] = value

    def pair_copy(way, slot, peer):
        return remote(
            pairs.at[slot], pairs.at[slot], kv_send.at[way, slot], kv_recv.at[slot], ctx=peer
        )

    pair_copy(0, place, up).start()
    pair_copy(1, place, down).start()
    pair_copy(2, place, twin).start()
    tail = remote(
        pairs.at[place, pl.ds(0, PAGE)], every.at[pl.ds(256, PAGE)],
        extra_send.at[0], extra_recv.at[0], ctx=jnp.maximum(ctx - 1, 0),
    )

    @pl.when(ctx > 0)
    def _():
        tail.start()

    query = turn(jnp.dot(normed[...], w_qkv_v[0], preferred_element_type=F32))
    queries[0] = query * jnp.asarray(1 / 16, BF16)

    def message(src, dst, number, peer):
        return remote(src, dst, extra_send.at[number], extra_recv.at[number], ctx=peer)

    ask = message(queries.at[0], queries.at[1], 1, across)
    asks = [message(queries.at[0], queries.at[2], 2 + i, 16 * i) for i in range(2)]
    show = message(pairs.at[place], pairs.at[16], 4, 16)
    gives = [
        message(reply.at[0], reply.at[2], 5, across),
        message(weight.at[0], weight.at[2], 6, across),
    ]
    back = 7 + 2 * z
    helps = [
        remote(reply.at[1], reply.at[3 + z], extra_send.at[7], extra_recv.at[back], ctx=32),
        remote(weight.at[1], weight.at[3 + z], extra_send.at[8], extra_recv.at[back + 1], ctx=32),
    ]

    @pl.when(z == 1)
    def _():
        ask.start()

    @pl.when(is_helped)
    def _():
        asks[1].start()
        show.start()
        asks[0].start()

    best[...] = jnp.full(best.shape, -jnp.inf, F32)
    total[...] = jnp.zeros(total.shape, F32)
    acc[...] = jnp.zeros(acc.shape, F32)
    q_place = lax.broadcasted_iota(jnp.int32, (ROWS, ROWS), 0)
    k_place = lax.broadcasted_iota(jnp.int32, (ROWS, ROWS), 1)

    def attend(which, slot, visible):
        scores = lax.dot_general(
            queries[which], pairs[slot, :, 0:256], (((1,), (1,)), ((), ())),
            preferred_element_type=F32,
        )
        scores = jnp.where(visible, scores, -jnp.inf)
        before = best[which]
        newest = jnp.maximum(before, jnp.max(scores, axis=-1, keepdims=True))
        rescale = jnp.exp(before - newest)
        weights = jnp.exp(scores - jnp.concatenate([newest, newest], axis=1)).astype(BF16)
        total[which] = total[which] * rescale + jnp.sum(
            weights.astype(F32), axis=-1, keepdims=True
        )
        acc[which] = acc[which] * jnp.concatenate([rescale, rescale], axis=1) + jnp.dot(
            weights, pairs[slot, :, 256:512], preferred_element_type=F32
        )
        best[which] = newest

    def visit(slot):
        bound = jnp.where((slot == 0) & (z == 0), length, 0)

        def one(which, carry):
            @pl.when(
                ((which == 0) & (slot < place))
                | ((which == 1) & (z == 0))
                | ((which == 2) & is_helper)
            )
            def _():
                attend(which, slot, k_place >= bound)

            return carry

        lax.fori_loop(0, 3, one, 0)

    own_bound = jnp.where(local == 0, length, 0)
    causal = k_place <= q_place
    attend(0, place, causal & ((k_place >= own_bound) == (q_place >= own_bound)))

    def here(slot):
        pair_copy(0, slot, up).wait_recv()

    @pl.when(ctx < 63)
    def _():
        tail.wait_recv()

    @pl.when(ctx == 63)
    def _():
        every[256:384, :] = jnp.zeros((PAGE, 512), BF16)

    shifts = [0] * 5
    counts = [0] * 5
    start = 0
    token = ctx * ROWS
    for prompt in range(3):
        size = lengths[prompt]
        head = jnp.maximum(token - start + PAGE - 1, 0) // PAGE
        for number in range(2):
            page = head + number
            row = start + page * PAGE - token
            valid = (row < ROWS) & (page * PAGE < size)
            entry = pages[prompt, jnp.minimum(page, 63)] % 5
            for slot in range(5):
                hit = valid & (entry == slot)
                shifts[slot] = shifts[slot] + jnp.where(hit, row, 0)
                counts[slot] = counts[slot] + jnp.where(hit, jnp.minimum(size - page * PAGE, PAGE), 0)
        start = start + size
    to_row = lax.broadcasted_iota(jnp.int32, (PAGE, 384), 0)
    from_row = lax.broadcasted_iota(jnp.int32, (PAGE, 384), 1)
    for slot in range(5):
        placing = (from_row == to_row + shifts[slot]) & (to_row < counts[slot])
        placing = jnp.where(placing, 1.0, 0.0).astype(BF16)
        cache[slot] = jnp.dot(placing, every[...], preferred_element_type=F32).astype(BF16)

    @pl.when(z == 0)
    def _():
        ask.wait_recv()

    @pl.when(ctx == 0)
    def _():
        asks[0].wait_recv()

    @pl.when(ctx == 16)
    def _():
        asks[1].wait_recv()
        show.wait_recv()
        attend(2, 16, causal)

    visit(place)
    here(place + 1 - 2 * core)
    visit(place + 1 - 2 * core)

    def spot(step):
        return ((y + pick(step, OFFSETS) + 8) % 8) * 2

    def event(step, carry):
        slot = spot(step) + core
        here(slot)

        @pl.when((step == 1) | (step == 3))
        def _():
            pair_copy(0, slot, up).start()

        @pl.when((step == 2) | (step == 4))
        def _():
            pair_copy(1, slot, down).start()

        @pl.when(step == 5)
        def _():
            half_copy(0, slot, up).start()

        @pl.when(step == 6)
        def _():
            half_copy(1, slot, down).start()

        pair_copy(2, slot, twin).start()
        visit(slot)
        beside = spot(step) + 1 - core
        here(beside)
        visit(beside)
        return carry

    def half_copy(way, slot, peer):
        rows = pl.ds(way * 128, 128)
        return remote(
            pairs.at[slot, rows], pairs.at[slot, rows],
            far_send.at[way], far_recv.at[way], ctx=peer,
        )

    lax.fori_loop(1, 7, event, 0)
    opposite = ((y + 4) % 8) * 2
    half_copy(0, opposite + core, up).wait_recv()
    half_copy(1, opposite + core, down).wait_recv()
    pair_copy(2, opposite + core, twin).start()
    visit(opposite + core)
    here(opposite + 1 - core)
    visit(opposite + 1 - core)

    def wide(value):
        return jnp.concatenate([value, value], axis=1)

    def hand_back(which, copies):
        reply[which - 1] = (acc[which] / wide(total[which])).astype(BF16)
        weight[which - 1] = jnp.transpose(best[which] + jnp.log(total[which]))[0:8]
        for copy in copies:
            copy.start()

    @pl.when(z == 0)
    def _():
        hand_back(1, gives)

    @pl.when(is_helper)
    def _():
        hand_back(2, helps)

    def logs(number):
        return jnp.transpose(jnp.tile(weight[number], (16, 1)))

    result = acc[0] / wide(total[0])
    attended[...] = result.astype(BF16)

    def blend(one, one_log, two, two_log):
        most = jnp.maximum(one_log, two_log)
        one_part, two_part = jnp.exp(one_log - most), jnp.exp(two_log - most)
        share = one_part / (one_part + two_part)
        other_share = two_part / (one_part + two_part)
        return one * wide(share) + two * wide(other_share)

    @pl.when(z == 1)
    def _():
        for copy in gives:
            copy.wait_recv()
        mixed = blend(
            acc[0] / wide(total[0]), best[0] + jnp.log(total[0]), reply[2].astype(F32), logs(2)
        )
        attended[...] = mixed.astype(BF16)

    @pl.when(is_helped)
    def _():
        for number in range(2):
            remote(
                reply.at[1], reply.at[3 + number],
                extra_send.at[7], extra_recv.at[7 + 2 * number], ctx=0,
            ).wait_recv()
            remote(
                weight.at[1], weight.at[3 + number],
                extra_send.at[8], extra_recv.at[8 + 2 * number], ctx=0,
            ).wait_recv()
        mixed = blend(reply[3].astype(F32), logs(3), reply[4].astype(F32), logs(4))
        rows = lax.broadcasted_iota(jnp.int32, (ROWS, 256), 0)
        attended[...] = jnp.where(
            rows < length, mixed, attended[...].astype(F32)
        ).astype(BF16)

    copies_in[5].wait()

    @pl.loop(0, 8)
    def _(b):
        cols = pl.ds(pl.multiple_of(b * 256, 256), 256)
        terms[b] = jnp.dot(
            attended[...], w_out_v[:, cols], preferred_element_type=F32
        ).astype(BF16)

    def sum_copy(number, src, dst, peer):
        return remote(src, dst, rs_send.at[number], rs_recv.at[number], tp=peer)

    first_ups, first_downs = [], []
    for k in range(2):
        side = (1 - half if k == 0 else half) * 4
        far = side + (x + 2) % 4
        first_ups.append(sum_copy(4 * k, terms.at[far, top], first.at[k, top], x_up))
        first_downs.append(
            sum_copy(4 * k + 1, terms.at[far, bottom], first.at[k, bottom], x_down)
        )
        first_ups[k].start()
        first_downs[k].start()
    seconds = []
    for k in range(2):
        side = (1 - half if k == 0 else half) * 4
        to_up, to_down = side + (x + 1) % 4, side + (x + 3) % 4
        first_ups[k].wait_recv()
        terms[to_up, top] = (
            terms[to_up, top].astype(F32) + first[k, top].astype(F32)
        ).astype(BF16)
        one = sum_copy(4 * k + 2, terms.at[to_up], second.at[k, 0], x_up)
        one.start()
        first_downs[k].wait_recv()
        terms[to_down, bottom] = (
            terms[to_down, bottom].astype(F32) + first[k, bottom].astype(F32)
        ).astype(BF16)
        two = sum_copy(4 * k + 3, terms.at[to_down], second.at[k, 1], x_down)
        two.start()
        seconds.append((one, two))

    def summed(k):
        side = (1 - half if k == 0 else half) * 4
        for copy in seconds[k]:
            copy.wait_recv()
        return (
            terms[side + x].astype(F32) + second[k, 0].astype(F32) + second[k, 1].astype(F32)
        )

    last[0] = summed(0).astype(BF16)
    final = sum_copy(8, last.at[0, top], last.at[1, top], mirror)
    aside = remote(last.at[0, bottom], relay.at[1], rs_send.at[9], relay_recv.at[1], **along_z(7))
    onward = remote(
        relay.at[1], last.at[1, bottom], rs_send.at[10], rs_recv.at[9], **along_z(5)
    )
    aside.start()
    final.start()
    aside.wait_recv()
    onward.start()
    kept = summed(1)
    final.wait_recv()
    onward.wait_recv()
    out[...] = (kept + last[1].astype(F32)).astype(BF16)

    for copy in first_ups + first_downs + [c for pair in seconds for c in pair] + [final, aside, onward]:
        copy.wait_send()

    @pl.when(ctx > 0)
    def _():
        tail.wait_send()

    @pl.when(z == 1)
    def _():
        ask.wait_send()

    @pl.when(is_helped)
    def _():
        for copy in asks + [show]:
            copy.wait_send()

    @pl.when(z == 0)
    def _():
        for copy in gives:
            copy.wait_send()

    @pl.when(is_helper)
    def _():
        for copy in helps:
            copy.wait_send()

    pair_copy(0, place, up).wait_send()
    pair_copy(1, place, down).wait_send()
    pair_copy(2, place, twin).wait_send()
    for step in range(1, 7):
        slot = spot(step) + core
        if step in (1, 3):
            pair_copy(0, slot, up).wait_send()
        if step in (2, 4):
            pair_copy(1, slot, down).wait_send()
        if step in (5, 6):
            half_copy(step - 5, slot, up).wait_send()
        pair_copy(2, slot, twin).wait_send()
    pair_copy(2, opposite + core, twin).wait_send()


def per_device(hidden_in, ln_gain, ln_bias, w_qkv, w_out, segment_ids, prompt_lengths, page_table):
    inverse = np.float32(10000.0) ** -(np.arange(0, 64, 2, dtype=np.float32) / np.float32(64))
    inverse = np.tile(inverse.astype(np.float32), 4)[None, :]
    vmem = pl.BlockSpec(memory_space=pltpu.VMEM)
    smem = pl.BlockSpec(memory_space=pltpu.SMEM)
    held = pl.BlockSpec(memory_space=pl.ANY)
    dma = pltpu.SemaphoreType.DMA
    attn_out, cache = pl.pallas_call(
        kernel,
        out_shape=(
            jax.ShapeDtypeStruct((ROWS, 256), BF16),
            jax.ShapeDtypeStruct((5, PAGE, 512), BF16),
        ),
        in_specs=[smem, smem] + [held] * 6,
        out_specs=(vmem, vmem),
        scratch_shapes=[
            pltpu.VMEM((ROWS, 256), BF16),
            pltpu.VMEM((1, 2048), F32),
            pltpu.VMEM((1, 2048), F32),
            pltpu.VMEM((1, 128), F32),
            pltpu.VMEM((ROWS, 128), F32),
            pltpu.VMEM((ROWS, 128), F32),
            pltpu.VMEM((8, ROWS, 256), BF16),
            pltpu.VMEM((ROWS, 2048), BF16),
            pltpu.VMEM((3, 2048, 256), BF16),
            pltpu.VMEM((256, 2048), BF16),
            pltpu.VMEM((3, ROWS, 256), BF16),
            pltpu.VMEM((17, ROWS, 512), BF16),
            pltpu.VMEM((384, 512), BF16),
            pltpu.VMEM((3, ROWS, 128), F32),
            pltpu.VMEM((3, ROWS, 128), F32),
            pltpu.VMEM((3, ROWS, 256), F32),
            pltpu.VMEM((5, ROWS, 256), BF16),
            pltpu.VMEM((5, 8, 256), F32),
            pltpu.VMEM((ROWS, 256), BF16),
            pltpu.VMEM((8, ROWS, 256), BF16),
            pltpu.VMEM((2, ROWS, 256), BF16),
            pltpu.VMEM((2, 2, ROWS, 256), BF16),
            pltpu.VMEM((2, ROWS, 256), BF16),
            pltpu.VMEM((2, 128, 256), BF16),
            dma((2,)),
            dma((6,)),
            dma((13,)),
            dma((8, 2)),
            dma((3, 16)),
            dma((16,)),
            dma((2,)),
            dma((2,)),
            dma((11,)),
            dma((11,)),
            dma((11,)),
            dma((10,)),
        ],
        compiler_params=pltpu.CompilerParams(
            collective_id=0, has_side_effects=True, vmem_limit_bytes=62 * 1024 * 1024
        ),
    )(
        prompt_lengths, page_table, hidden_in, ln_gain.reshape(1, -1), ln_bias.reshape(1, -1),
        jnp.asarray(inverse), w_qkv, w_out,
    )
    return (attn_out, cache.reshape(5, PAGE, 2, 256))


def solution(mesh):
    return jax.shard_map(
        per_device,
        mesh=mesh,
        in_specs=(P("ctx", "tp"), P(), P(), P(None, None, "tp"), P("tp", None), P("ctx"), P(), P()),
        out_specs=(P("ctx", "tp"), P("ctx", None, None, "tp")),
        check_vma=False,
    )
```

```python
import jax
import numpy as np
import jax.numpy as jnp
from jax import lax
from jax.experimental import pallas as pl
from jax.experimental.pallas import tpu as pltpu
from jax.sharding import PartitionSpec as P

HD = 256
PAGE = 128
ROWS = 256
GROUP = 32
EPSILON = 1e-05
TURN = (6.28125, 0.00193500518798828125, 3.0197e-07)
MESH = pl.DeviceIdType.MESH
F32 = jnp.float32
BF16 = jnp.bfloat16

OFFSETS = (0, -1, 1, -2, 2, -3, 3)


def pick(step, table):
    value = 0
    for place, entry in enumerate(table):
        if entry != 0:
            value = value + jnp.where(step == place, entry, 0)
    return value


def remote(src, dst, send, recv, **where):
    return pltpu.make_async_remote_copy(
        src_ref=src, dst_ref=dst, send_sem=send, recv_sem=recv, device_id=where, device_id_type=MESH
    )


def kernel(
    lengths, pages, hidden_h, gain_h, bias_h, inverse_h, w_qkv, w_out,
    out, cache,
    hidden, gain, bias, inverse, cosine, sine, gathered, normed, w_qkv_v, w_out_v, queries, pairs, every, best, total, acc,
    reply, weight, attended, terms, first, second, last,
    local_sem, ag_send, ag_recv, kv_send, kv_recv, far_send, far_recv, extra_send, extra_recv, rs_send, rs_recv,
):
    ctx = lax.axis_index("ctx")
    tp = lax.axis_index("tp")
    group = ctx // GROUP
    local = ctx % GROUP
    z = local // 16
    y = (local // 2) % 8
    core = local % 2
    base = group * GROUP
    half = tp // 4
    x = tp % 4
    up = base + z * 16 + ((y + 1) % 8) * 2 + core
    down = base + z * 16 + ((y + 7) % 8) * 2 + core
    twin = base + z * 16 + y * 2 + (1 - core)
    across = base + (1 - z) * 16 + y * 2 + core
    x_up = half * 4 + (x + 1) % 4
    x_down = half * 4 + (x + 3) % 4
    x_far = half * 4 + (x + 2) % 4
    mirror = (1 - half) * 4 + x
    place = local % 16
    is_helper = (ctx == 0) | (ctx == 16)
    is_helped = ctx == 32

    copies_in = [
        pltpu.make_async_copy(source, target, local_sem.at[number])
        for number, (source, target) in enumerate((
            (hidden_h, hidden), (inverse_h, inverse), (gain_h, gain), (bias_h, bias),
            (w_qkv, w_qkv_v), (w_out, w_out_v),
        ))
    ]
    for copy in copies_in:
        copy.start()

    barrier = pltpu.get_barrier_semaphore()
    for peer in (up, down, twin, across):
        pl.semaphore_signal(barrier, inc=1, device_id={"ctx": peer}, device_id_type=MESH)
    for peer in (x_up, x_down, mirror):
        pl.semaphore_signal(barrier, inc=1, device_id={"tp": peer}, device_id_type=MESH)

    @pl.when(ctx > 0)
    def _():
        pl.semaphore_signal(barrier, inc=1, device_id={"ctx": ctx - 1}, device_id_type=MESH)

    @pl.when(ctx < 63)
    def _():
        pl.semaphore_signal(barrier, inc=1, device_id={"ctx": ctx + 1}, device_id_type=MESH)

    @pl.when(is_helper)
    def _():
        pl.semaphore_signal(barrier, inc=1, device_id={"ctx": 32}, device_id_type=MESH)

    @pl.when(is_helped)
    def _():
        for peer in (0, 16):
            pl.semaphore_signal(barrier, inc=1, device_id={"ctx": peer}, device_id_type=MESH)

    pl.semaphore_wait(
        barrier,
        7 + jnp.where(ctx > 0, 1, 0) + jnp.where(ctx < 63, 1, 0)
        + jnp.where(is_helper, 1, 0) + jnp.where(is_helped, 2, 0),
    )

    top, bottom = pl.ds(0, 128), pl.ds(128, 128)

    def feature_copy(number, src, slot, part, peer, rows=None):
        dst = gathered.at[slot] if rows is None else gathered.at[slot, rows]
        return remote(src, dst, ag_send.at[number], ag_recv.at[slot, part], tp=peer)

    copies_in[0].wait()
    own_z = feature_copy(0, hidden.at[top], tp, 0, mirror, top)
    own_rest = feature_copy(9, hidden.at[bottom], tp, 1, mirror, bottom)
    own_up = feature_copy(1, hidden, tp, 0, x_up)
    own_down = feature_copy(2, hidden, tp, 0, x_down)
    for copy in (own_z, own_rest, own_up, own_down):
        copy.start()
    gathered[tp] = hidden[...]
    sent = [own_z, own_rest, own_up, own_down]

    copies_in[1].wait()
    index = ctx * ROWS + lax.broadcasted_iota(jnp.int32, (ROWS, 128), 0)
    lane = lax.broadcasted_iota(jnp.int32, (ROWS, 128), 1)
    length = lengths[0]
    both = length + lengths[1]
    places = index - jnp.where(index < length, 0, jnp.where(index < both, length, both))
    angles = places.astype(F32) * inverse[...]
    turns = jnp.floor(angles * F32(0.15915494309189535) + 0.5)
    for part in TURN:
        angles = angles - turns * F32(part)
    cosine[...] = jnp.where(lane < 64, jnp.cos(angles), 1.0)
    sine[...] = jnp.where(
        lane < 32, -jnp.sin(angles), jnp.where(lane < 64, jnp.sin(angles), 0.0)
    )

    def arrived(slot, part, rows=None):
        dst = gathered.at[slot] if rows is None else gathered.at[slot, rows]
        remote(dst, dst, ag_send.at[0], ag_recv.at[slot, part], tp=mirror).wait_recv()

    def send(copy):
        copy.start()
        sent.append(copy)

    arrived(x_down, 0)
    send(feature_copy(3, gathered.at[x_down, top], x_down, 0, x_up, top))
    arrived(x_up, 0)
    send(feature_copy(4, gathered.at[x_up, bottom], x_up, 1, x_down, bottom))
    other = (1 - half) * 4
    beyond_down, beyond_up = other + (x + 3) % 4, other + (x + 1) % 4
    beyond_far = other + (x + 2) % 4
    arrived(mirror, 0, top)
    send(feature_copy(5, gathered.at[mirror, top], mirror, 0, x_up, top))
    send(feature_copy(6, gathered.at[mirror, top], mirror, 0, x_down, top))
    arrived(beyond_down, 0, top)
    send(feature_copy(7, gathered.at[beyond_down, top], beyond_down, 0, x_up, top))
    arrived(mirror, 1, bottom)
    send(feature_copy(11, gathered.at[mirror, bottom], mirror, 1, x_up, bottom))
    send(feature_copy(12, gathered.at[mirror, bottom], mirror, 1, x_down, bottom))
    arrived(beyond_up, 1, bottom)
    send(feature_copy(8, gathered.at[beyond_up, bottom], beyond_up, 1, x_down, bottom))
    for slot in (x_far, beyond_far):
        arrived(slot, 0, top)
        arrived(slot, 1, bottom)
    arrived(beyond_down, 1, bottom)
    arrived(beyond_up, 0, top)
    for copy in sent:
        copy.wait_send()

    copies_in[2].wait()
    copies_in[3].wait()
    @pl.loop(0, ROWS // 32)
    def _(step):
        rows = pl.ds(pl.multiple_of(step * 32, 32), 32)
        blocks = [gathered[b, rows, :].astype(F32) for b in range(8)]
        average = jnp.sum(sum(blocks), axis=-1, keepdims=True) / 2048
        centered = [block - average for block in blocks]
        spread = jnp.sum(sum(c * c for c in centered), axis=-1, keepdims=True) / 2048
        scale = lax.rsqrt(spread + EPSILON)
        for b in range(8):
            cols = pl.ds(b * 256, 256)
            value = centered[b] * scale * gain[:, cols] + bias[:, cols]
            normed[rows, cols] = value.astype(BF16)

    copies_in[4].wait()

    def turn(value):
        lead = value[:, :128]
        turned = jnp.where(lane < 32, pltpu.roll(lead, 96, 1), pltpu.roll(lead, 32, 1))
        lead = lead * cosine[...] + turned * sine[...]
        return jnp.concatenate([lead, value[:, 128:]], axis=1).astype(BF16)

    key = turn(jnp.dot(normed[...], w_qkv_v[1], preferred_element_type=F32))
    pairs[place, :, 0:256] = key
    every[0:256, 0:256] = key
    value = jnp.dot(normed[...], w_qkv_v[2], preferred_element_type=F32).astype(BF16)
    pairs[place, :, 256:512] = value
    every[0:256, 256:512] = value

    def pair_copy(way, slot, peer):
        return remote(
            pairs.at[slot], pairs.at[slot], kv_send.at[way, slot], kv_recv.at[slot], ctx=peer
        )

    pair_copy(0, place, up).start()
    pair_copy(1, place, down).start()
    pair_copy(2, place, twin).start()
    tail = remote(
        pairs.at[place, pl.ds(0, PAGE)], every.at[pl.ds(256, PAGE)],
        extra_send.at[0], extra_recv.at[0], ctx=jnp.maximum(ctx - 1, 0),
    )

    @pl.when(ctx > 0)
    def _():
        tail.start()

    query = turn(jnp.dot(normed[...], w_qkv_v[0], preferred_element_type=F32))
    queries[0] = query * jnp.asarray(1 / 16, BF16)

    def message(src, dst, number, peer):
        return remote(src, dst, extra_send.at[number], extra_recv.at[number], ctx=peer)

    ask = message(queries.at[0], queries.at[1], 1, across)
    asks = [message(queries.at[0], queries.at[2], 2 + i, 16 * i) for i in range(2)]
    show = message(pairs.at[place], pairs.at[16], 4, 16)
    gives = [
        message(reply.at[0], reply.at[2], 5, across),
        message(weight.at[0], weight.at[2], 6, across),
    ]
    back = 7 + 2 * z
    helps = [
        remote(reply.at[1], reply.at[3 + z], extra_send.at[7], extra_recv.at[back], ctx=32),
        remote(weight.at[1], weight.at[3 + z], extra_send.at[8], extra_recv.at[back + 1], ctx=32),
    ]

    @pl.when(z == 1)
    def _():
        ask.start()

    @pl.when(is_helped)
    def _():
        asks[1].start()
        show.start()
        asks[0].start()

    best[...] = jnp.full(best.shape, -jnp.inf, F32)
    total[...] = jnp.zeros(total.shape, F32)
    acc[...] = jnp.zeros(acc.shape, F32)
    q_place = lax.broadcasted_iota(jnp.int32, (ROWS, ROWS), 0)
    k_place = lax.broadcasted_iota(jnp.int32, (ROWS, ROWS), 1)

    def attend(which, slot, visible):
        scores = lax.dot_general(
            queries[which], pairs[slot, :, 0:256], (((1,), (1,)), ((), ())),
            preferred_element_type=F32,
        )
        scores = jnp.where(visible, scores, -jnp.inf)
        before = best[which]
        newest = jnp.maximum(before, jnp.max(scores, axis=-1, keepdims=True))
        rescale = jnp.exp(before - newest)
        weights = jnp.exp(scores - jnp.concatenate([newest, newest], axis=1)).astype(BF16)
        total[which] = total[which] * rescale + jnp.sum(
            weights.astype(F32), axis=-1, keepdims=True
        )
        acc[which] = acc[which] * jnp.concatenate([rescale, rescale], axis=1) + jnp.dot(
            weights, pairs[slot, :, 256:512], preferred_element_type=F32
        )
        best[which] = newest

    def visit(slot):
        bound = jnp.where((slot == 0) & (z == 0), length, 0)

        def one(which, carry):
            @pl.when(
                ((which == 0) & (slot < place))
                | ((which == 1) & (z == 0))
                | ((which == 2) & is_helper)
            )
            def _():
                attend(which, slot, k_place >= bound)

            return carry

        lax.fori_loop(0, 3, one, 0)

    own_bound = jnp.where(local == 0, length, 0)
    causal = k_place <= q_place
    attend(0, place, causal & ((k_place >= own_bound) == (q_place >= own_bound)))

    def here(slot):
        pair_copy(0, slot, up).wait_recv()

    @pl.when(ctx < 63)
    def _():
        tail.wait_recv()

    @pl.when(ctx == 63)
    def _():
        every[256:384, :] = jnp.zeros((PAGE, 512), BF16)

    shifts = [0] * 5
    counts = [0] * 5
    start = 0
    token = ctx * ROWS
    for prompt in range(3):
        size = lengths[prompt]
        head = jnp.maximum(token - start + PAGE - 1, 0) // PAGE
        for number in range(2):
            page = head + number
            row = start + page * PAGE - token
            valid = (row < ROWS) & (page * PAGE < size)
            entry = pages[prompt, jnp.minimum(page, 63)] % 5
            for slot in range(5):
                hit = valid & (entry == slot)
                shifts[slot] = shifts[slot] + jnp.where(hit, row, 0)
                counts[slot] = counts[slot] + jnp.where(hit, jnp.minimum(size - page * PAGE, PAGE), 0)
        start = start + size
    to_row = lax.broadcasted_iota(jnp.int32, (PAGE, 384), 0)
    from_row = lax.broadcasted_iota(jnp.int32, (PAGE, 384), 1)
    for slot in range(5):
        placing = (from_row == to_row + shifts[slot]) & (to_row < counts[slot])
        placing = jnp.where(placing, 1.0, 0.0).astype(BF16)
        cache[slot] = jnp.dot(placing, every[...], preferred_element_type=F32).astype(BF16)

    @pl.when(z == 0)
    def _():
        ask.wait_recv()

    @pl.when(ctx == 0)
    def _():
        asks[0].wait_recv()

    @pl.when(ctx == 16)
    def _():
        asks[1].wait_recv()
        show.wait_recv()
        attend(2, 16, causal)

    visit(place)
    here(place + 1 - 2 * core)
    visit(place + 1 - 2 * core)

    def spot(step):
        return ((y + pick(step, OFFSETS) + 8) % 8) * 2

    def event(step, carry):
        slot = spot(step) + core
        here(slot)

        @pl.when((step == 1) | (step == 3))
        def _():
            pair_copy(0, slot, up).start()

        @pl.when((step == 2) | (step == 4))
        def _():
            pair_copy(1, slot, down).start()

        @pl.when(step == 5)
        def _():
            half_copy(0, slot, up).start()

        @pl.when(step == 6)
        def _():
            half_copy(1, slot, down).start()

        pair_copy(2, slot, twin).start()
        visit(slot)
        beside = spot(step) + 1 - core
        here(beside)
        visit(beside)
        return carry

    def half_copy(way, slot, peer):
        rows = pl.ds(way * 128, 128)
        return remote(
            pairs.at[slot, rows], pairs.at[slot, rows],
            far_send.at[way], far_recv.at[way], ctx=peer,
        )

    lax.fori_loop(1, 7, event, 0)
    opposite = ((y + 4) % 8) * 2
    half_copy(0, opposite + core, up).wait_recv()
    half_copy(1, opposite + core, down).wait_recv()
    pair_copy(2, opposite + core, twin).start()
    visit(opposite + core)
    here(opposite + 1 - core)
    visit(opposite + 1 - core)

    def wide(value):
        return jnp.concatenate([value, value], axis=1)

    def hand_back(which, copies):
        reply[which - 1] = (acc[which] / wide(total[which])).astype(BF16)
        weight[which - 1] = jnp.transpose(best[which] + jnp.log(total[which]))[0:8]
        for copy in copies:
            copy.start()

    @pl.when(z == 0)
    def _():
        hand_back(1, gives)

    @pl.when(is_helper)
    def _():
        hand_back(2, helps)

    def logs(number):
        return jnp.transpose(jnp.tile(weight[number], (16, 1)))

    result = acc[0] / wide(total[0])
    attended[...] = result.astype(BF16)

    def blend(one, one_log, two, two_log):
        most = jnp.maximum(one_log, two_log)
        one_part, two_part = jnp.exp(one_log - most), jnp.exp(two_log - most)
        share = one_part / (one_part + two_part)
        other_share = two_part / (one_part + two_part)
        return one * wide(share) + two * wide(other_share)

    @pl.when(z == 1)
    def _():
        for copy in gives:
            copy.wait_recv()
        mixed = blend(
            acc[0] / wide(total[0]), best[0] + jnp.log(total[0]), reply[2].astype(F32), logs(2)
        )
        attended[...] = mixed.astype(BF16)

    @pl.when(is_helped)
    def _():
        for number in range(2):
            remote(
                reply.at[1], reply.at[3 + number],
                extra_send.at[7], extra_recv.at[7 + 2 * number], ctx=0,
            ).wait_recv()
            remote(
                weight.at[1], weight.at[3 + number],
                extra_send.at[8], extra_recv.at[8 + 2 * number], ctx=0,
            ).wait_recv()
        mixed = blend(reply[3].astype(F32), logs(3), reply[4].astype(F32), logs(4))
        rows = lax.broadcasted_iota(jnp.int32, (ROWS, 256), 0)
        attended[...] = jnp.where(
            rows < length, mixed, attended[...].astype(F32)
        ).astype(BF16)

    copies_in[5].wait()

    @pl.loop(0, 8)
    def _(b):
        cols = pl.ds(pl.multiple_of(b * 256, 256), 256)
        terms[b] = jnp.dot(
            attended[...], w_out_v[:, cols], preferred_element_type=F32
        ).astype(BF16)

    def sum_copy(number, src, dst, peer):
        return remote(src, dst, rs_send.at[number], rs_recv.at[number], tp=peer)

    first_ups, first_downs = [], []
    for k in range(2):
        side = (1 - half if k == 0 else half) * 4
        far = side + (x + 2) % 4
        first_ups.append(sum_copy(4 * k, terms.at[far, top], first.at[k, top], x_up))
        first_downs.append(
            sum_copy(4 * k + 1, terms.at[far, bottom], first.at[k, bottom], x_down)
        )
        first_ups[k].start()
        first_downs[k].start()
    seconds = []
    for k in range(2):
        side = (1 - half if k == 0 else half) * 4
        to_up, to_down = side + (x + 1) % 4, side + (x + 3) % 4
        first_ups[k].wait_recv()
        terms[to_up, top] = (
            terms[to_up, top].astype(F32) + first[k, top].astype(F32)
        ).astype(BF16)
        one = sum_copy(4 * k + 2, terms.at[to_up], second.at[k, 0], x_up)
        one.start()
        first_downs[k].wait_recv()
        terms[to_down, bottom] = (
            terms[to_down, bottom].astype(F32) + first[k, bottom].astype(F32)
        ).astype(BF16)
        two = sum_copy(4 * k + 3, terms.at[to_down], second.at[k, 1], x_down)
        two.start()
        seconds.append((one, two))

    def summed(k):
        side = (1 - half if k == 0 else half) * 4
        for copy in seconds[k]:
            copy.wait_recv()
        return (
            terms[side + x].astype(F32) + second[k, 0].astype(F32) + second[k, 1].astype(F32)
        )

    last[0] = summed(0).astype(BF16)
    final = sum_copy(8, last.at[0], last.at[1], mirror)
    final.start()
    kept = summed(1)
    final.wait_recv()
    out[...] = (kept + last[1].astype(F32)).astype(BF16)

    for copy in first_ups + first_downs + [c for pair in seconds for c in pair] + [final]:
        copy.wait_send()

    @pl.when(ctx > 0)
    def _():
        tail.wait_send()

    @pl.when(z == 1)
    def _():
        ask.wait_send()

    @pl.when(is_helped)
    def _():
        for copy in asks + [show]:
            copy.wait_send()

    @pl.when(z == 0)
    def _():
        for copy in gives:
            copy.wait_send()

    @pl.when(is_helper)
    def _():
        for copy in helps:
            copy.wait_send()

    pair_copy(0, place, up).wait_send()
    pair_copy(1, place, down).wait_send()
    pair_copy(2, place, twin).wait_send()
    for step in range(1, 7):
        slot = spot(step) + core
        if step in (1, 3):
            pair_copy(0, slot, up).wait_send()
        if step in (2, 4):
            pair_copy(1, slot, down).wait_send()
        if step in (5, 6):
            half_copy(step - 5, slot, up).wait_send()
        pair_copy(2, slot, twin).wait_send()
    pair_copy(2, opposite + core, twin).wait_send()


def per_device(hidden_in, ln_gain, ln_bias, w_qkv, w_out, segment_ids, prompt_lengths, page_table):
    inverse = np.float32(10000.0) ** -(np.arange(0, 64, 2, dtype=np.float32) / np.float32(64))
    inverse = np.tile(inverse.astype(np.float32), 4)[None, :]
    vmem = pl.BlockSpec(memory_space=pltpu.VMEM)
    smem = pl.BlockSpec(memory_space=pltpu.SMEM)
    held = pl.BlockSpec(memory_space=pl.ANY)
    dma = pltpu.SemaphoreType.DMA
    attn_out, cache = pl.pallas_call(
        kernel,
        out_shape=(
            jax.ShapeDtypeStruct((ROWS, 256), BF16),
            jax.ShapeDtypeStruct((5, PAGE, 512), BF16),
        ),
        in_specs=[smem, smem] + [held] * 6,
        out_specs=(vmem, vmem),
        scratch_shapes=[
            pltpu.VMEM((ROWS, 256), BF16),
            pltpu.VMEM((1, 2048), F32),
            pltpu.VMEM((1, 2048), F32),
            pltpu.VMEM((1, 128), F32),
            pltpu.VMEM((ROWS, 128), F32),
            pltpu.VMEM((ROWS, 128), F32),
            pltpu.VMEM((8, ROWS, 256), BF16),
            pltpu.VMEM((ROWS, 2048), BF16),
            pltpu.VMEM((3, 2048, 256), BF16),
            pltpu.VMEM((256, 2048), BF16),
            pltpu.VMEM((3, ROWS, 256), BF16),
            pltpu.VMEM((17, ROWS, 512), BF16),
            pltpu.VMEM((384, 512), BF16),
            pltpu.VMEM((3, ROWS, 128), F32),
            pltpu.VMEM((3, ROWS, 128), F32),
            pltpu.VMEM((3, ROWS, 256), F32),
            pltpu.VMEM((5, ROWS, 256), BF16),
            pltpu.VMEM((5, 8, 256), F32),
            pltpu.VMEM((ROWS, 256), BF16),
            pltpu.VMEM((8, ROWS, 256), BF16),
            pltpu.VMEM((2, ROWS, 256), BF16),
            pltpu.VMEM((2, 2, ROWS, 256), BF16),
            pltpu.VMEM((2, ROWS, 256), BF16),
            dma((6,)),
            dma((13,)),
            dma((8, 2)),
            dma((3, 16)),
            dma((16,)),
            dma((2,)),
            dma((2,)),
            dma((11,)),
            dma((11,)),
            dma((9,)),
            dma((9,)),
        ],
        compiler_params=pltpu.CompilerParams(
            collective_id=0, has_side_effects=True, vmem_limit_bytes=62 * 1024 * 1024
        ),
    )(
        prompt_lengths, page_table, hidden_in, ln_gain.reshape(1, -1), ln_bias.reshape(1, -1),
        jnp.asarray(inverse), w_qkv, w_out,
    )
    return (attn_out, cache.reshape(5, PAGE, 2, 256))


def solution(mesh):
    return jax.shard_map(
        per_device,
        mesh=mesh,
        in_specs=(P("ctx", "tp"), P(), P(), P(None, None, "tp"), P("tp", None), P("ctx"), P(), P()),
        out_specs=(P("ctx", "tp"), P("ctx", None, None, "tp")),
        check_vma=False,
    )
```
